32 devices in a mesh: frame: 16 (over z, x, core), coil: 2 (over y).
Axes of the slice: x: 2, y: 2, z: 4, core: 2. Of those that a mesh axis runs over, the one named last changes fastest.
Arguments:
- kspace: bfloat16 [16, 64, 256, 512], P('frame', 'coil'), may hold values from -6 to 6
- sens: bfloat16 [64, 256, 512], P('coil'), may hold values from -0.5 to 0.5
- mask: int32 [16, 64, 256], P('frame', 'coil'), may hold values 0 or 1
- image: float32 [16, 256, 512], P('frame', 'coil'), may hold values from -6 to 6
- w_first: bfloat16 [3, 3, 3, 64, 2], replicated, may hold values from -0.875 to 0.875
- b_first: float32 [64], replicated, may hold values from -3 to 3
- w_mid: bfloat16 [3, 3, 3, 64, 64], replicated, may hold values from -0.15625 to 0.15625
- b_mid: float32 [64], replicated, may hold values from -3 to 3
- w_last: bfloat16 [3, 3, 3, 2, 64], replicated, may hold values from -0.15625 to 0.15625
Outputs:
- recon: float32 [16, 256, 512], P('frame', 'coil')
The draws below stay inside these ranges and needn't reach their ends.
Inputs may be any that keep to these rules, and one draw needn't show every extreme that they name: mask is 1 on the acquired phase-encoding lines of a frame and coil and 0 on the others.
All inputs are finite; a program needn't handle non-finite values. No bound on the sum of `mask` on one device may be relied on, other than what follows from the above.
Results may differ from the reference program's by a relative error of at most 0.006.
Values may be sent and summed in bfloat16 or wider, within the bound.
No kernel may reach another device: no remote copies, remote signals or barrier semaphores. Data moves between devices by JAX's collectives and lax.ppermute only.
A program may use at most 192 MiB of HBM per device.

```python
import math
import jax
import jax.numpy as jnp
from jax import lax

NR = 256
NC = 256
COILS = 64
CH = 64
OUTER = 1
DSTEPS = 1
FRAMES = 16


def place_ends(values, key, least, largest):
    extent = values.shape
    spot = [jax.random.randint(jax.random.fold_in(key, axis), (), 0, extent[axis]) for axis in range(len(extent))]
    values = values.at[tuple(spot)].set(least)
    longest = extent.index(max(extent))
    spot[longest] = (spot[longest] + 1) % extent[longest]
    return values.at[tuple(spot)].set(largest)


def levels(rng, extent, pieces, smallest, top_value):
    factor_of = 1.0
    for dim, parts in pieces:
        draws = jax.random.uniform(jax.random.fold_in(jax.random.fold_in(rng, 6), dim), (parts,), jnp.float32, smallest / len(pieces), top_value / len(pieces))
        factor_of = factor_of * jnp.repeat(jnp.exp(draws), extent[dim] // parts).reshape((-1,) + (1,) * (len(extent) - 1 - dim))
    return factor_of


def scatter_about(rng, dims, width, reach, pieces=(), held_as=jnp.bfloat16):
    loudness = levels(rng, dims, pieces, -0.22, 0.18) if pieces else 1.0
    values = jax.random.normal(rng, dims, jnp.float32) * width * loudness
    return jnp.minimum(jnp.maximum(values, -reach), reach).astype(held_as)


def setup_inputs(seed: int = 0) -> dict:
    key_of = jax.random.split(jax.random.key(seed), 10)
    return {
        "kspace": scatter_about(key_of[0], (FRAMES, COILS, NR, 2 * NC), 1.0, 6.0, ((0, 16), (1, 2))),
        "sens": scatter_about(key_of[1], (COILS, NR, 2 * NC), (2 * COILS) ** -0.5, 0.5, ((0, 2),)),
        "mask": place_ends((jax.random.randint(key_of[2], (FRAMES, COILS, NR), 0, 3) < 1).astype(jnp.int32), jax.random.fold_in(key_of[2], 1), 0, 1),
        "image": scatter_about(key_of[3], (FRAMES, NR, 2 * NC), 1.0, 6.0, ((0, 16), (1, 2)), jnp.float32),
        "w_first": scatter_about(key_of[4], (3, 3, 3, CH, 2), 54 ** -0.5, 0.875),
        "b_first": scatter_about(key_of[5], (CH,), 0.5, 3.0, (), jnp.float32),
        "w_mid": scatter_about(key_of[6], (3, 3, 3, CH, CH), (27 * CH) ** -0.5, 0.15625),
        "b_mid": scatter_about(key_of[7], (CH,), 0.5, 3.0, (), jnp.float32),
        "w_last": scatter_about(key_of[8], (3, 3, 3, 2, CH), (27 * CH) ** -0.5, 0.15625),
    }


step_size = 1.0

def dft_parts(order):
    indices = jnp.arange(order, dtype=jnp.int32)
    phases = indices[:, None] * indices[None, :] % order
    angles = phases.astype(jnp.float32) * (2.0 * math.pi / order)
    factor = 1.0 / math.sqrt(order)
    return ((jnp.cos(angles) * factor).astype(jnp.bfloat16), (-jnp.sin(angles) * factor).astype(jnp.bfloat16))

def column_tables(real_part, imag_part):
    ahead = jnp.concatenate([jnp.concatenate([real_part, imag_part], 1), jnp.concatenate([-imag_part, real_part], 1)], 0)
    behind = jnp.concatenate([jnp.concatenate([real_part, -imag_part], 1), jnp.concatenate([imag_part, real_part], 1)], 0)
    return (ahead, behind)

def swapped(values):
    half_width = values.shape[-1] // 2
    return jnp.concatenate([-values[..., half_width:], values[..., :half_width]], -1)

def complex_mul(first, second):
    half_width = first.shape[-1] // 2
    first_re, first_im = (first[..., :half_width], first[..., half_width:])
    second_re, second_im = (second[..., :half_width], second[..., half_width:])
    return jnp.concatenate([first_re * second_re - first_im * second_im, first_re * second_im + first_im * second_re], -1)

def conj_mul(first, second):
    half_width = first.shape[-1] // 2
    first_re, first_im = (first[..., :half_width], first[..., half_width:])
    second_re, second_im = (second[..., :half_width], second[..., half_width:])
    return jnp.concatenate([first_re * second_re + first_im * second_im, first_re * second_im - first_im * second_re], -1)

def data_frame(image_now, kspace, sampled, sens, row_real, row_imag, ahead, behind):
    f32 = jnp.float32
    image_low = image_now.astype(jnp.bfloat16)
    coil_image = complex_mul(sens.astype(f32), image_low.astype(f32)[None]).astype(jnp.bfloat16)
    cols_spectrum = jnp.einsum('crm,mn->crn', coil_image.astype(f32), ahead.astype(f32)).astype(jnp.bfloat16)
    row_ahead = jnp.concatenate([row_real, row_imag], 1)
    stacked = jnp.concatenate([cols_spectrum, swapped(cols_spectrum)], 1)
    estimate = jnp.einsum('kr,crn->ckn', row_ahead.astype(f32), stacked.astype(f32))
    misfit = (sampled.astype(f32)[..., None] * (estimate - kspace.astype(f32))).astype(jnp.bfloat16)
    back_cols = jnp.einsum('ckm,mn->ckn', misfit.astype(f32), behind.astype(f32)).astype(jnp.bfloat16)
    row_behind = jnp.concatenate([row_real, -row_imag], 1)
    stacked_back = jnp.concatenate([back_cols, swapped(back_cols)], 1)
    back_image = jnp.einsum('rk,ckn->crn', row_behind.astype(f32), stacked_back.astype(f32))
    gradient = lax.optimization_barrier(jnp.sum(conj_mul(sens.astype(f32), back_image), 0))
    return image_now - step_size * gradient

def conv_layer(padded, weight):
    frames = padded.shape[0] - 2
    rows = padded.shape[1] - 2
    out_chan = weight.shape[3]
    in_chan = weight.shape[4]
    window = jnp.concatenate([padded[tap_frame:tap_frame + frames, tap_row:tap_row + rows] for tap_frame in range(3) for tap_row in range(3)], 2)
    matrix = jnp.transpose(weight, (2, 3, 0, 1, 4)).reshape(3 * out_chan, 9 * in_chan)
    taps_out = jnp.einsum('km,frmn->frkn', matrix.astype(jnp.float32), window.astype(jnp.float32))
    left_taps = taps_out[:, :, :out_chan]
    centre = taps_out[:, :, out_chan:2 * out_chan]
    right_taps = taps_out[:, :, 2 * out_chan:]
    zeros_col = jnp.zeros_like(left_taps[..., :1])
    return centre + jnp.concatenate([zeros_col, left_taps[..., :-1]], -1) + jnp.concatenate([right_taps[..., 1:], zeros_col], -1)

def conv_frames(hidden, weight):
    padded = jnp.pad(hidden, ((1, 1), (1, 1), (0, 0), (0, 0)))

    def one_frame(frame_idx):
        block = lax.dynamic_slice_in_dim(padded, frame_idx, 3, 0)
        return conv_layer(block, weight)[0]
    return lax.map(one_frame, jnp.arange(hidden.shape[0], dtype=jnp.int32))

def denoise(image_now, w_first, b_first, w_mid, b_mid, w_last):
    frames, rows, double = image_now.shape
    hidden = image_now.reshape(frames, rows, 2, double // 2).astype(jnp.bfloat16)
    first = jax.nn.relu(conv_frames(hidden, w_first) + b_first[None, None, :, None]).astype(jnp.bfloat16)
    second = jax.nn.relu(conv_frames(first, w_mid) + b_mid[None, None, :, None]).astype(jnp.bfloat16)
    update = conv_frames(second, w_last)
    return image_now + update.reshape(frames, rows, double)

def reference(kspace, sens, mask, image, w_first, b_first, w_mid, b_mid, w_last):
    row_real, row_imag = dft_parts(sens.shape[1])
    col_real, col_imag = dft_parts(sens.shape[2] // 2)
    ahead, behind = column_tables(col_real, col_imag)
    image_now = image
    for sweep_idx in range(OUTER):
        for inner_idx in range(DSTEPS):
            image_now = lax.map(lambda items: data_frame(items[0], items[1], items[2], sens, row_real, row_imag, ahead, behind), (image_now, kspace, mask))
        image_now = denoise(image_now, w_first, b_first, w_mid, b_mid, w_last)
    return image_now
```

```python
import functools
import math

import jax
import jax.numpy as jnp
import numpy as np
from jax import lax
from jax.experimental import pallas as pl
from jax.experimental.pallas import tpu as pltpu
from jax.sharding import PartitionSpec as P

F32 = jnp.float32
BF16 = jnp.bfloat16

step_size = 1.0
RIM = 8
SLOT = 32


def dft_parts(order):
    indices = jnp.arange(order, dtype=jnp.int32)
    phases = indices[:, None] * indices[None, :] % order
    angles = phases.astype(F32) * (2.0 * math.pi / order)
    factor = 1.0 / math.sqrt(order)
    return (
        (jnp.cos(angles) * factor).astype(BF16),
        (-jnp.sin(angles) * factor).astype(BF16),
    )


def side_by_side(real_part, imag_part):
    return jnp.concatenate(
        [
            jnp.concatenate([real_part, imag_part], 1),
            jnp.concatenate([-imag_part, real_part], 1),
        ],
        0,
    )


def data_kernel(
    coils_at_once,
    chunk,
    where_ref,
    image_ref,
    others_ref,
    kspace_ref,
    sens_ref,
    mask_ref,
    col_ahead_ref,
    col_behind_ref,
    row_ahead_ref,
    row_behind_ref,
    own_ref,
    send_ref,
    full_ref,
    acc_ref,
    coil_ref,
    spec_ref,
    esti_ref,
):
    groups = others_ref.shape[0] + 1
    own_rows = image_ref.shape[0]
    n_rows, double = full_ref.shape
    half = double // 2
    me = where_ref[0]
    step = pl.program_id(0)

    @pl.when(step == 0)
    def _():
        acc_ref[...] = jnp.zeros_like(acc_ref)
        mine = pl.multiple_of(me * own_rows, RIM)
        acc_ref[pl.ds(pl.multiple_of(mine + RIM, RIM), own_rows), :] = image_ref[...]
        full_ref[pl.ds(mine, own_rows), :] = image_ref[...].astype(BF16).astype(F32)
        for hop in range(1, groups):
            theirs = pl.multiple_of(lax.rem(me + groups - hop, groups) * own_rows, RIM)
            full_ref[pl.ds(theirs, own_rows), :] = others_ref[hop - 1].astype(F32)

    for coil in range(coils_at_once):
        for start in range(0, n_rows, chunk):
            rows = slice(start, start + chunk)
            sens_re = sens_ref[coil, rows, :half].astype(F32)
            sens_im = sens_ref[coil, rows, half:].astype(F32)
            x_re, x_im = full_ref[rows, :half], full_ref[rows, half:]
            out = slice(coil * n_rows + start, coil * n_rows + start + chunk)
            coil_ref[out, :half] = (sens_re * x_re - sens_im * x_im).astype(BF16)
            coil_ref[out, half:] = (sens_re * x_im + sens_im * x_re).astype(BF16)
    spec_ref[...] = jnp.dot(
        coil_ref[...], col_ahead_ref[...], preferred_element_type=F32
    ).astype(BF16)
    for coil in range(coils_at_once):
        block = slice(coil * n_rows, (coil + 1) * n_rows)
        stacked = jnp.concatenate([spec_ref[block, :half], spec_ref[block, half:]], 0)
        esti_ref[coil] = jnp.dot(row_ahead_ref[...], stacked, preferred_element_type=F32)
    for coil in range(coils_at_once):
        sampled = jnp.broadcast_to(mask_ref[coil].astype(F32), (128, n_rows)).T
        for start in range(0, n_rows, chunk):
            rows = slice(start, start + chunk)
            out = slice(coil * n_rows + start, coil * n_rows + start + chunk)
            line = jnp.concatenate([sampled[rows]] * (half // 128), 1)
            coil_ref[out, :half] = (
                line * (esti_ref[coil, rows, :] - kspace_ref[coil, rows, :half].astype(F32))
            ).astype(BF16)
            lower = slice(n_rows + start, n_rows + start + chunk)
            coil_ref[out, half:] = (
                line * (esti_ref[coil, lower, :] - kspace_ref[coil, rows, half:].astype(F32))
            ).astype(BF16)
    spec_ref[...] = jnp.dot(
        coil_ref[...], col_behind_ref[...], preferred_element_type=F32
    ).astype(BF16)
    for coil in range(coils_at_once):
        block = slice(coil * n_rows, (coil + 1) * n_rows)
        stacked = jnp.concatenate([spec_ref[block, :half], spec_ref[block, half:]], 0)
        esti_ref[coil] = jnp.dot(row_behind_ref[...], stacked, preferred_element_type=F32)
    for start in range(0, n_rows, chunk):
        rows = slice(start, start + chunk)
        place = slice(RIM + start, RIM + start + chunk)
        lower = slice(n_rows + start, n_rows + start + chunk)
        total_re, total_im = acc_ref[place, :half], acc_ref[place, half:]
        for coil in range(coils_at_once):
            sens_re = sens_ref[coil, rows, :half].astype(F32) * step_size
            sens_im = sens_ref[coil, rows, half:].astype(F32) * step_size
            back_re, back_im = esti_ref[coil, rows, :], esti_ref[coil, lower, :]
            total_re = total_re - (sens_re * back_re + sens_im * back_im)
            total_im = total_im - (sens_re * back_im - sens_im * back_re)
        acc_ref[place, :half] = total_re
        acc_ref[place, half:] = total_im

    @pl.when(step == pl.num_programs(0) - 1)
    def _():
        window = own_rows + 2 * RIM
        own_ref[...] = acc_ref[pl.ds(pl.multiple_of(me * own_rows, RIM), window), :]
        for hop in range(1, groups):
            theirs = pl.multiple_of(lax.rem(me + hop, groups) * own_rows, RIM)
            send_ref[hop - 1] = acc_ref[pl.ds(theirs, window), :]


def data_step(image, kspace, sens, mask, here, groups):
    own_rows, double = image.shape
    coils, n_rows, _ = sens.shape
    half = double // 2
    coils_at_once = 2
    shift = lambda hop: [(i, (i + hop) % groups) for i in range(groups)]
    low = image.astype(BF16)
    others = jnp.stack([lax.ppermute(low, "coil", shift(hop)) for hop in range(1, groups)])
    row_re, row_im = dft_parts(n_rows)
    col_re, col_im = dft_parts(half)
    tables = (
        side_by_side(col_re, col_im),
        side_by_side(col_re, -col_im),
        side_by_side(row_re, row_im).T,
        side_by_side(row_re, -row_im).T,
    )
    window = own_rows + 2 * RIM
    whole = lambda a: pl.BlockSpec(a.shape, lambda i: (0,) * a.ndim)
    per_coil = lambda a: pl.BlockSpec(
        (coils_at_once,) + a.shape[1:], lambda i: (i,) + (0,) * (a.ndim - 1)
    )
    mask = mask.reshape(coils, 1, n_rows)
    own, send = pl.pallas_call(
        functools.partial(data_kernel, coils_at_once, 32),
        grid=(coils // coils_at_once,),
        in_specs=[
            pl.BlockSpec(memory_space=pltpu.SMEM),
            whole(image),
            whole(others),
            per_coil(kspace),
            per_coil(sens),
            per_coil(mask),
        ]
        + [whole(table) for table in tables],
        out_specs=[
            pl.BlockSpec((window, double), lambda i: (0, 0)),
            pl.BlockSpec((groups - 1, window, double), lambda i: (0, 0, 0)),
        ],
        out_shape=[
            jax.ShapeDtypeStruct((window, double), F32),
            jax.ShapeDtypeStruct((groups - 1, window, double), F32),
        ],
        scratch_shapes=[
            pltpu.VMEM((n_rows, double), F32),
            pltpu.VMEM((n_rows + 2 * RIM, double), F32),
            pltpu.VMEM((coils_at_once * n_rows, double), BF16),
            pltpu.VMEM((coils_at_once * n_rows, double), BF16),
            pltpu.VMEM((coils_at_once, 2 * n_rows, half), F32),
        ],
        cost_estimate=pl.CostEstimate(
            flops=32 * coils * n_rows * n_rows * half,
            bytes_accessed=4 * coils * n_rows * double,
            transcendentals=0,
        ),
        name="data_step",
    )(here, image, others, kspace, sens, mask, *tables)
    for hop in range(1, groups):
        own = own + lax.ppermute(send[hop - 1], "coil", shift(hop))
    return own


def first_selector(channels_in):
    taps = 27 * channels_in
    select = np.zeros((4, 3, taps + 3, 6 * SLOT), np.float32)
    for row in range(4):
        for frame in range(3):
            for a in range(3):
                for b in range(3):
                    for e in range(3):
                        for c in range(channels_in):
                            tap = ((a * 3 + b) * 3 + e) * channels_in + c
                            at = ((frame + a) * channels_in + c) * 3 + e
                            select[row, frame, tap, (row + b) * SLOT + at] = 1.0
            for part in range(3):
                at = (part // 2) * SLOT + SLOT - 2 + part % 2
                select[row, frame, taps + part, at] = 1.0
    return select.reshape(12, taps + 3, 6 * SLOT)


def three_parts(values):
    high = lax.reduce_precision(values, 8, 7)
    rest = values - high
    middle = lax.reduce_precision(rest, 8, 7)
    return jnp.stack([high, middle, rest - middle], -1).astype(BF16)


def shifted(values, amount):
    width = values.shape[-1]
    lane = lax.broadcasted_iota(jnp.int32, values.shape, 1)
    if amount > 0:
        return jnp.where(lane == 0, 0.0, pltpu.roll(values, 1, 1))
    return jnp.where(lane == width - 1, 0.0, pltpu.roll(values, width - 1, 1))


def denoise_kernel(
    where_ref,
    x_ref,
    f0_ref,
    f1_ref,
    f2_ref,
    f3_ref,
    f4_ref,
    w1_ref,
    select_ref,
    wm_ref,
    bm_ref,
    wl_ref,
    before_ref,
    base_ref,
    after_ref,
    slab_ref,
    wide_ref,
    h1_ref,
    h2_ref,
):
    window, double = x_ref.shape
    half = double // 2
    rows = window - 2 * RIM
    out_chan = w1_ref.shape[0]
    per_row = 3 * out_chan
    first_group, last_group = where_ref[0], where_ref[1]

    for frame, ref in enumerate((f0_ref, f1_ref, f2_ref, f3_ref, f4_ref)):
        for c in range(2):
            plane = ref[:, c * half : (c + 1) * half].astype(F32)
            for e, moved in enumerate((shifted(plane, 1), plane, shifted(plane, -1))):
                for j in range(half // 128):
                    slab_ref[j, pl.ds((frame * 2 + c) * 3 + e, window, stride=SLOT), :] = (
                        moved[:, j * 128 : (j + 1) * 128]
                    )
    ones = jnp.ones((window, 128), F32)
    for spare in (SLOT - 2, SLOT - 1):
        for j in range(half // 128):
            slab_ref[j, pl.ds(spare, window, stride=SLOT), :] = ones
    for row in range(4):
        for frame in range(3):
            band = jnp.dot(
                w1_ref[...], select_ref[row * 3 + frame], preferred_element_type=F32
            )
            if frame != 1:
                band = band * where_ref[2 + frame // 2].astype(F32)
            at = (row * 3 + frame) * out_chan
            wide_ref[at : at + out_chan, :] = band.astype(BF16)

    def first(q, carry):
        source = pl.multiple_of((4 * q + RIM - 3) * SLOT, SLOT)
        taps = jnp.concatenate(
            [slab_ref[j, pl.ds(source, 6 * SLOT), :] for j in range(half // 128)], 1
        ).astype(BF16)
        made = jnp.dot(wide_ref[...], taps, preferred_element_type=F32)
        target = pl.multiple_of(4 * q * per_row, per_row)
        h1_ref[pl.ds(target, 4 * per_row), :] = jnp.maximum(made, 0.0).astype(BF16)
        return carry

    lax.fori_loop(0, (rows + 4) // 4, first, 0)
    edge = jnp.zeros((2 * per_row, half), BF16)

    @pl.when(first_group == 1)
    def _():
        h1_ref[: 2 * per_row, :] = edge

    @pl.when(last_group == 1)
    def _():
        h1_ref[(rows + 2) * per_row :, :] = edge

    both = 2 * out_chan
    bias = jnp.broadcast_to(bm_ref[...], (both, half))

    def mid(p, carry):
        source = pl.multiple_of(2 * p * per_row, 2 * per_row)
        taps = h1_ref[pl.ds(source, 4 * per_row), :]
        made = jnp.dot(wm_ref[...], taps, preferred_element_type=F32)
        total = (
            made[both : 2 * both]
            + shifted(made[:both], 1)
            + shifted(made[2 * both :], -1)
            + bias
        )
        target = pl.multiple_of(p * both, both)
        h2_ref[pl.ds(target, both), :] = jnp.maximum(total, 0.0).astype(BF16)
        return carry

    lax.fori_loop(0, (rows + 2) // 2, mid, 0)
    edge2 = jnp.zeros((out_chan, half), BF16)

    @pl.when(first_group == 1)
    def _():
        h2_ref[:out_chan, :] = edge2

    @pl.when(last_group == 1)
    def _():
        h2_ref[(rows + 1) * out_chan :, :] = edge2

    def last(q, carry):
        source = pl.multiple_of(8 * q * out_chan, 8 * out_chan)
        taps = h2_ref[pl.ds(source, 10 * out_chan), :]
        made = jnp.dot(wl_ref[...], taps, preferred_element_type=F32)
        total = made[48:96] + shifted(made[:48], 1) + shifted(made[96:], -1)
        at = pl.ds(pl.multiple_of(8 * q, 8), 8)
        for c in range(2):
            lanes = slice(c * half, (c + 1) * half)
            piece = lambda a: total[(a * 2 + c) * 8 : (a * 2 + c) * 8 + 8]
            after_ref[at, lanes] = piece(0)
            base_ref[at, lanes] = (
                x_ref[pl.ds(pl.multiple_of(8 * q + RIM, 8), 8), lanes] + piece(1)
            )
            before_ref[at, lanes] = piece(2)
        return carry

    lax.fori_loop(0, rows // 8, last, 0)


def denoise(x, w_first, b_first, w_mid, b_mid, w_last, frame, frames, group, groups):
    window, double = x.shape
    rows, half = window - 2 * RIM, double // 2
    out_chan = w_mid.shape[3]
    hidden = x.astype(BF16)
    near = {0: hidden}
    for by in (1, 2):
        near[-by] = lax.ppermute(hidden, "frame", [(i, i + by) for i in range(frames - by)])
        near[by] = lax.ppermute(hidden, "frame", [(i + by, i) for i in range(frames - by)])
    where = jnp.stack(
        [group == 0, group == groups - 1, frame > 0, frame < frames - 1]
    ).astype(jnp.int32)
    w1 = jnp.concatenate(
        [
            jnp.transpose(w_first, (3, 0, 1, 2, 4)).reshape(out_chan, -1),
            three_parts(b_first),
        ],
        1,
    )
    select = jnp.asarray(first_selector(w_first.shape[4]), BF16)
    mid = jnp.transpose(w_mid, (2, 3, 1, 0, 4)).reshape(3, out_chan, -1)
    spare = 3 * out_chan
    wm = jnp.stack(
        [
            jnp.pad(mid, ((0, 0), (0, 0), (0, spare))),
            jnp.pad(mid, ((0, 0), (0, 0), (spare, 0))),
        ],
        1,
    ).reshape(6 * out_chan, -1)
    bm = jnp.concatenate([b_mid, b_mid])[:, None]
    last = jnp.transpose(w_last, (2, 0, 3, 1, 4)).reshape(18, -1)
    wl = jnp.stack(
        [jnp.pad(last, ((0, 0), (r * out_chan, (7 - r) * out_chan))) for r in range(8)], 1
    ).reshape(144, -1)
    vmem = pl.BlockSpec(memory_space=pltpu.VMEM)
    out = jax.ShapeDtypeStruct((rows, double), F32)
    before, base, after = pl.pallas_call(
        denoise_kernel,
        in_specs=[pl.BlockSpec(memory_space=pltpu.SMEM)] + [vmem] * 11,
        out_specs=[vmem] * 3,
        out_shape=[out] * 3,
        scratch_shapes=[
            pltpu.VMEM((half // 128, window * SLOT, 128), F32),
            pltpu.VMEM((12 * out_chan, 6 * SLOT), BF16),
            pltpu.VMEM(((rows + 4) * 3 * out_chan, half), BF16),
            pltpu.VMEM(((rows + 2) * out_chan, half), BF16),
        ],
        cost_estimate=pl.CostEstimate(
            flops=2 * (rows + 2) * half * 192 * 1152,
            bytes_accessed=4 * window * double * 5,
            transcendentals=0,
        ),
        name="denoise",
    )(where, x, *[near[by] for by in (-2, -1, 0, 1, 2)], w1, select, wm, bm, wl)
    upward = [(i, i + 1) for i in range(frames - 1)]
    downward = [(i + 1, i) for i in range(frames - 1)]
    return (
        base + lax.ppermute(after, "frame", upward) + lax.ppermute(before, "frame", downward)
    )


def shards(kspace, sens, mask, image, w_first, b_first, w_mid, b_mid, w_last):
    frame, group = lax.axis_index("frame"), lax.axis_index("coil")
    frames, groups = lax.axis_size("frame"), lax.axis_size("coil")
    here = group.astype(jnp.int32)[None]
    x = data_step(image[0], kspace[0], sens, mask[0], here, groups)
    return denoise(x, w_first, b_first, w_mid, b_mid, w_last, frame, frames, group, groups)[None]


def solution(mesh):
    in_specs = (
        P("frame", "coil", None, None),
        P("coil", None, None),
        P("frame", "coil", None),
        P("frame", "coil", None),
        P(),
        P(),
        P(),
        P(),
        P(),
    )
    out_specs = P("frame", "coil", None)
    return jax.shard_map(shards, mesh=mesh, in_specs=in_specs, out_specs=out_specs, check_vma=False)
```

```python
import functools
import math

import jax
import jax.numpy as jnp
import numpy as np
from jax import lax
from jax.experimental import pallas as pl
from jax.experimental.pallas import tpu as pltpu
from jax.sharding import PartitionSpec as P

F32 = jnp.float32
BF16 = jnp.bfloat16

step_size = 1.0
RIM = 8
SLOT = 32


def dft_parts(order):
    indices = np.arange(order)
    angles = (indices[:, None] * indices[None, :] % order).astype(np.float32)
    angles = angles * np.float32(2.0 * math.pi / order)
    factor = np.float32(1.0 / math.sqrt(order))
    return jnp.asarray(np.stack([np.cos(angles) * factor, -np.sin(angles) * factor]), BF16)


def put_table(ref, top_left, top_right, low_left, low_right):
    half = top_left.shape[0]
    ref[:half, :half] = top_left
    ref[:half, half:] = top_right
    ref[half:, :half] = low_left
    ref[half:, half:] = low_right


def data_kernel(
    coils_at_once,
    chunk,
    where_ref,
    image_ref,
    others_ref,
    kspace_ref,
    sens_ref,
    mask_ref,
    cols_ref,
    lines_ref,
    own_ref,
    send_ref,
    full_ref,
    acc_ref,
    coil_ref,
    spec_ref,
    esti_ref,
    miss_ref,
    back_ref,
    bimg_ref,
    col_ahead_ref,
    col_behind_ref,
    row_ahead_ref,
    row_behind_ref,
):
    groups = others_ref.shape[0] + 1
    own_rows = image_ref.shape[0]
    n_rows, double = full_ref.shape
    half = double // 2
    me = where_ref[0]
    step = pl.program_id(0)

    @pl.when(step == 0)
    def _():
        for ref, ahead_ref, behind_ref in (
            (cols_ref, col_ahead_ref, col_behind_ref),
            (lines_ref, row_behind_ref, row_ahead_ref),
        ):
            real, imag = ref[0], ref[1]
            put_table(ahead_ref, real, imag, -imag, real)
            put_table(behind_ref, real, -imag, imag, real)
        acc_ref[...] = jnp.zeros_like(acc_ref)
        mine = pl.multiple_of(me * own_rows, RIM)
        acc_ref[pl.ds(pl.multiple_of(mine + RIM, RIM), own_rows), :] = image_ref[...]
        full_ref[pl.ds(mine, own_rows), :] = image_ref[...].astype(BF16).astype(F32)
        for hop in range(1, groups):
            theirs = pl.multiple_of(lax.rem(me + groups - hop, groups) * own_rows, RIM)
            full_ref[pl.ds(theirs, own_rows), :] = others_ref[hop - 1].astype(F32)

    for coil in range(coils_at_once):
        for start in range(0, n_rows, chunk):
            rows = slice(start, start + chunk)
            sens_re = sens_ref[coil, rows, :half].astype(F32)
            sens_im = sens_ref[coil, rows, half:].astype(F32)
            x_re, x_im = full_ref[rows, :half], full_ref[rows, half:]
            out = slice(coil * n_rows + start, coil * n_rows + start + chunk)
            coil_ref[out, :half] = (sens_re * x_re - sens_im * x_im).astype(BF16)
            coil_ref[out, half:] = (sens_re * x_im + sens_im * x_re).astype(BF16)
    spec_ref[...] = jnp.dot(
        coil_ref[...], col_ahead_ref[...], preferred_element_type=F32
    ).astype(BF16)
    for coil in range(coils_at_once):
        block = slice(coil * n_rows, (coil + 1) * n_rows)
        stacked = jnp.concatenate([spec_ref[block, :half], spec_ref[block, half:]], 0)
        esti_ref[coil] = jnp.dot(row_ahead_ref[...], stacked, preferred_element_type=F32)
    for coil in range(coils_at_once):
        line = mask_ref[pl.ds(step * coils_at_once + coil, 1), :].astype(F32)
        sampled = jnp.broadcast_to(line, (128, n_rows)).T
        for start in range(0, n_rows, chunk):
            rows = slice(start, start + chunk)
            out = slice(coil * n_rows + start, coil * n_rows + start + chunk)
            line = jnp.concatenate([sampled[rows]] * (half // 128), 1)
            miss_ref[out, :half] = (
                line * (esti_ref[coil, rows, :] - kspace_ref[coil, rows, :half].astype(F32))
            ).astype(BF16)
            lower = slice(n_rows + start, n_rows + start + chunk)
            miss_ref[out, half:] = (
                line * (esti_ref[coil, lower, :] - kspace_ref[coil, rows, half:].astype(F32))
            ).astype(BF16)
    back_ref[...] = jnp.dot(
        miss_ref[...], col_behind_ref[...], preferred_element_type=F32
    ).astype(BF16)
    for coil in range(coils_at_once):
        block = slice(coil * n_rows, (coil + 1) * n_rows)
        stacked = jnp.concatenate([back_ref[block, :half], back_ref[block, half:]], 0)
        bimg_ref[coil] = jnp.dot(row_behind_ref[...], stacked, preferred_element_type=F32)
    for start in range(0, n_rows, chunk):
        rows = slice(start, start + chunk)
        place = slice(RIM + start, RIM + start + chunk)
        lower = slice(n_rows + start, n_rows + start + chunk)
        total_re, total_im = acc_ref[place, :half], acc_ref[place, half:]
        for coil in range(coils_at_once):
            sens_re = sens_ref[coil, rows, :half].astype(F32) * step_size
            sens_im = sens_ref[coil, rows, half:].astype(F32) * step_size
            back_re, back_im = bimg_ref[coil, rows, :], bimg_ref[coil, lower, :]
            total_re = total_re - (sens_re * back_re + sens_im * back_im)
            total_im = total_im - (sens_re * back_im - sens_im * back_re)
        acc_ref[place, :half] = total_re
        acc_ref[place, half:] = total_im

    @pl.when(step == pl.num_programs(0) - 1)
    def _():
        window = own_rows + 2 * RIM
        own_ref[...] = acc_ref[pl.ds(pl.multiple_of(me * own_rows, RIM), window), :]
        for hop in range(1, groups):
            theirs = pl.multiple_of(lax.rem(me + hop, groups) * own_rows, RIM)
            send_ref[hop - 1] = acc_ref[pl.ds(theirs, window), :].astype(BF16)


def data_step(image, kspace, sens, mask, here, groups):
    own_rows, double = image.shape
    coils, n_rows, _ = sens.shape
    half = double // 2
    coils_at_once = unrolled(coils, 4)
    shift = lambda hop: [(i, (i + hop) % groups) for i in range(groups)]
    low = image.astype(BF16)
    others = jnp.stack([lax.ppermute(low, "coil", shift(hop)) for hop in range(1, groups)])
    cols, lines = dft_parts(half), dft_parts(n_rows)
    window = own_rows + 2 * RIM
    whole = lambda a: pl.BlockSpec(a.shape, lambda i: (0,) * a.ndim)
    per_coil = lambda a: pl.BlockSpec(
        (coils_at_once,) + a.shape[1:], lambda i: (i,) + (0,) * (a.ndim - 1)
    )
    own, send = pl.pallas_call(
        functools.partial(data_kernel, coils_at_once, 32),
        grid=(coils // coils_at_once,),
        in_specs=[
            pl.BlockSpec(memory_space=pltpu.SMEM),
            whole(image),
            whole(others),
            per_coil(kspace),
            per_coil(sens),
            whole(mask),
            whole(cols),
            whole(lines),
        ],
        out_specs=[
            pl.BlockSpec((window, double), lambda i: (0, 0)),
            pl.BlockSpec((groups - 1, window, double), lambda i: (0, 0, 0)),
        ],
        out_shape=[
            jax.ShapeDtypeStruct((window, double), F32),
            jax.ShapeDtypeStruct((groups - 1, window, double), BF16),
        ],
        scratch_shapes=[
            pltpu.VMEM((n_rows, double), F32),
            pltpu.VMEM((n_rows + 2 * RIM, double), F32),
            pltpu.VMEM((coils_at_once * n_rows, double), BF16),
            pltpu.VMEM((coils_at_once * n_rows, double), BF16),
            pltpu.VMEM((coils_at_once, 2 * n_rows, half), F32),
            pltpu.VMEM((coils_at_once * n_rows, double), BF16),
            pltpu.VMEM((coils_at_once * n_rows, double), BF16),
            pltpu.VMEM((coils_at_once, 2 * n_rows, half), F32),
        ]
        + [pltpu.VMEM((double, double), BF16)] * 2
        + [pltpu.VMEM((2 * n_rows, 2 * n_rows), BF16)] * 2,
        compiler_params=pltpu.CompilerParams(vmem_limit_bytes=57 << 20),
        cost_estimate=pl.CostEstimate(
            flops=32 * coils * n_rows * n_rows * half,
            bytes_accessed=4 * coils * n_rows * double,
            transcendentals=0,
        ),
        name="data_step",
    )(here, image, others, kspace, sens, mask, cols, lines)
    for hop in range(1, groups):
        own = own + lax.ppermute(send[hop - 1], "coil", shift(hop)).astype(F32)
    return own


def first_selector(channels_in):
    taps = 27 * channels_in
    select = np.zeros((4, 3, 64, 6 * SLOT), np.float32)
    for row in range(4):
        for frame in range(3):
            for a in range(3):
                for b in range(3):
                    for e in range(3):
                        for c in range(channels_in):
                            tap = ((a * 3 + b) * 3 + e) * channels_in + c
                            at = ((frame + a) * channels_in + c) * 3 + e
                            select[row, frame, tap, (row + b) * SLOT + at] = 1.0
            for part in range(3):
                at = (part // 2) * SLOT + SLOT - 2 + part % 2
                select[row, frame, taps + part, at] = 1.0
    return select.reshape(12, 64, 6 * SLOT)


def interleaver():
    order = np.zeros((8 * SLOT, 8 * SLOT), np.float32)
    for row in range(8):
        for plane in range(SLOT):
            order[row * SLOT + plane, plane * 8 + row] = 1.0
    return order


def last_selector():
    select = np.zeros((3, 3, 3, 2, 8, 54), np.float32)
    for b in range(3):
        for e in range(3):
            for a in range(3):
                for c in range(2):
                    select[b, e, a, c, :, ((a * 3 + b) * 3 + e) * 2 + c] = 1.0
    return select.reshape(432, 54)


def unrolled(count, at_most):
    return max(d for d in range(1, at_most + 1) if count % d == 0)


def shifted(values, amount):
    width = values.shape[-1]
    lane = lax.broadcasted_iota(jnp.int32, values.shape, 1)
    if amount > 0:
        return jnp.where(lane == 0, 0.0, pltpu.roll(values, 1, 1))
    return jnp.where(lane == width - 1, 0.0, pltpu.roll(values, width - 1, 1))


def denoise_kernel(
    groups,
    frames,
    group_ref,
    frame_ref,
    x_ref,
    f0_ref,
    f1_ref,
    f2_ref,
    f3_ref,
    f4_ref,
    w1_ref,
    b1_ref,
    select_ref,
    order_ref,
    wmid_ref,
    bm_ref,
    wlast_ref,
    place_ref,
    before_ref,
    base_ref,
    after_ref,
    plane_ref,
    slab_ref,
    wide_ref,
    wm_ref,
    wl_ref,
    h1_ref,
    h2_ref,
):
    window, double = x_ref.shape
    half = double // 2
    rows = window - 2 * RIM
    out_chan = wmid_ref.shape[1]
    per_row = 3 * out_chan
    group, frame_now = group_ref[0], frame_ref[0]

    bias1 = b1_ref[...]
    high = bias1.astype(BF16).astype(F32)
    middle = (bias1 - high).astype(BF16).astype(F32)
    parts = [w1_ref[...].astype(F32), high, middle, bias1 - high - middle]
    spare = 64 - sum(part.shape[0] for part in parts)
    w1 = jnp.concatenate(parts + [jnp.zeros((spare, out_chan), F32)], 0).T.astype(BF16)
    inside = (frame_now > 0, None, frame_now < frames - 1)
    for row in range(4):
        for frame in range(3):
            band = jnp.dot(w1, select_ref[row * 3 + frame], preferred_element_type=F32)
            if inside[frame] is not None:
                band = band * jnp.where(inside[frame], 1.0, 0.0)
            at = (row * 3 + frame) * out_chan
            wide_ref[at : at + out_chan, :] = band.astype(BF16)
    nothing = jnp.zeros((out_chan, out_chan), BF16)
    for e in range(3):
        for row in range(2):
            blocks = [
                wmid_ref[(a * 3 + r - row) * 3 + e] if 0 <= r - row <= 2 else nothing
                for r in range(4)
                for a in range(3)
            ]
            at = (e * 2 + row) * out_chan
            wm_ref[at : at + out_chan, :] = jnp.concatenate(blocks, 1)
    picked = jnp.dot(place_ref[...], wlast_ref[...], preferred_element_type=F32)
    eight = lax.broadcasted_iota(jnp.int32, (144, out_chan), 0) & 7
    wl_ref[...] = jnp.concatenate(
        [
            sum(
                jnp.where(eight == r - b, picked[b * 144 : (b + 1) * 144], 0.0)
                for b in range(3)
            )
            for r in range(10)
        ],
        1,
    ).astype(BF16)
    for frame, ref in enumerate((f0_ref, f1_ref, f2_ref, f3_ref, f4_ref)):
        for c in range(2):
            plane = ref[:, c * half : (c + 1) * half].astype(F32)
            for e, moved in enumerate((shifted(plane, 1), plane, shifted(plane, -1))):
                plane_ref[(frame * 2 + c) * 3 + e] = moved
    ones = jnp.ones((16, half), F32)

    def interleave(block, carry):
        rows8 = pl.ds(pl.multiple_of(block * 8, 8), 8)
        planes = [plane_ref[k, rows8, :] for k in range(30)] + [ones]
        taps = jnp.concatenate(planes, 0).astype(BF16)
        made = jnp.dot(order_ref[...], taps, preferred_element_type=F32)
        slab_ref[pl.ds(pl.multiple_of(block * 8 * SLOT, 8 * SLOT), 8 * SLOT), :] = made.astype(BF16)
        return carry

    lax.fori_loop(0, window // 8, interleave, 0, unroll=unrolled(window // 8, 6))

    def first(q, carry):
        source = pl.multiple_of((4 * q + RIM - 3) * SLOT, SLOT)
        taps = slab_ref[pl.ds(source, 6 * SLOT), :]
        made = jnp.dot(wide_ref[...], taps, preferred_element_type=F32)
        target = pl.multiple_of(4 * q * per_row, per_row)
        h1_ref[pl.ds(target, 4 * per_row), :] = jnp.maximum(made, 0.0).astype(BF16)
        return carry

    lax.fori_loop(0, (rows + 4) // 4, first, 0, unroll=unrolled((rows + 4) // 4, 11))
    edge = jnp.zeros((2 * per_row, half), BF16)

    @pl.when(group == 0)
    def _():
        h1_ref[: 2 * per_row, :] = edge

    @pl.when(group == groups - 1)
    def _():
        h1_ref[(rows + 2) * per_row :, :] = edge

    both = 2 * out_chan
    bias = jnp.broadcast_to(bm_ref[...], (128, out_chan)).T
    bias = jnp.concatenate([bias] * 2, 0)
    bias = jnp.concatenate([bias] * (half // 128), 1)

    def mid(p, carry):
        source = pl.multiple_of(2 * p * per_row, 2 * per_row)
        taps = h1_ref[pl.ds(source, 4 * per_row), :]
        made = jnp.dot(wm_ref[...], taps, preferred_element_type=F32)
        total = (
            made[both : 2 * both]
            + shifted(made[:both], 1)
            + shifted(made[2 * both :], -1)
            + bias
        )
        target = pl.multiple_of(p * both, both)
        h2_ref[pl.ds(target, both), :] = jnp.maximum(total, 0.0).astype(BF16)
        return carry

    lax.fori_loop(0, (rows + 2) // 2, mid, 0, unroll=unrolled((rows + 2) // 2, 13))
    edge2 = jnp.zeros((out_chan, half), BF16)

    @pl.when(group == 0)
    def _():
        h2_ref[:out_chan, :] = edge2

    @pl.when(group == groups - 1)
    def _():
        h2_ref[(rows + 1) * out_chan :, :] = edge2

    def last(q, carry):
        source = pl.multiple_of(8 * q * out_chan, 8 * out_chan)
        taps = h2_ref[pl.ds(source, 10 * out_chan), :]
        made = jnp.dot(wl_ref[...], taps, preferred_element_type=F32)
        total = made[48:96] + shifted(made[:48], 1) + shifted(made[96:], -1)
        at = pl.ds(pl.multiple_of(8 * q, 8), 8)
        for c in range(2):
            lanes = slice(c * half, (c + 1) * half)
            piece = lambda a: total[(a * 2 + c) * 8 : (a * 2 + c) * 8 + 8]
            after_ref[at, lanes] = piece(0).astype(BF16)
            base_ref[at, lanes] = (
                x_ref[pl.ds(pl.multiple_of(8 * q + RIM, 8), 8), lanes] + piece(1)
            )
            before_ref[at, lanes] = piece(2).astype(BF16)
        return carry

    lax.fori_loop(0, rows // 8, last, 0, unroll=unrolled(rows // 8, 8))


def denoise(x, w_first, b_first, w_mid, b_mid, w_last, frame, frames, group, groups):
    window, double = x.shape
    rows, half = window - 2 * RIM, double // 2
    out_chan = w_mid.shape[3]
    hidden = x.astype(BF16)
    near = {0: hidden}
    for by in (1, 2):
        near[-by] = lax.ppermute(hidden, "frame", [(i, i + by) for i in range(frames - by)])
        near[by] = lax.ppermute(hidden, "frame", [(i + by, i) for i in range(frames - by)])
    weights = (
        jnp.transpose(w_first, (0, 1, 2, 4, 3)).reshape(-1, out_chan),
        b_first[None],
        jnp.asarray(first_selector(w_first.shape[4]), BF16),
        jnp.asarray(interleaver(), BF16),
        w_mid.reshape(-1, out_chan, out_chan),
        b_mid[None],
        w_last.reshape(-1, out_chan),
        jnp.asarray(last_selector(), BF16),
    )
    vmem = pl.BlockSpec(memory_space=pltpu.VMEM)
    smem = pl.BlockSpec(memory_space=pltpu.SMEM)
    out = lambda dtype: jax.ShapeDtypeStruct((rows, double), dtype)
    before, base, after = pl.pallas_call(
        functools.partial(denoise_kernel, groups, frames),
        in_specs=[smem] * 2 + [vmem] * 14,
        out_specs=[vmem] * 3,
        out_shape=[out(BF16), out(F32), out(BF16)],
        compiler_params=pltpu.CompilerParams(vmem_limit_bytes=44 << 20),
        scratch_shapes=[
            pltpu.VMEM((30, window, half), F32),
            pltpu.VMEM((window * SLOT, half), BF16),
            pltpu.VMEM((12 * out_chan, 6 * SLOT), BF16),
            pltpu.VMEM((6 * out_chan, 12 * out_chan), BF16),
            pltpu.VMEM((144, 10 * out_chan), BF16),
            pltpu.VMEM(((rows + 4) * 3 * out_chan, half), BF16),
            pltpu.VMEM(((rows + 2) * out_chan, half), BF16),
        ],
        cost_estimate=pl.CostEstimate(
            flops=2 * (rows + 2) * half * 192 * 1152,
            bytes_accessed=4 * window * double * 5,
            transcendentals=0,
        ),
        name="denoise",
    )(
        group.astype(jnp.int32)[None],
        frame.astype(jnp.int32)[None],
        x,
        *[near[by] for by in (-2, -1, 0, 1, 2)],
        *weights,
    )
    upward = [(i, i + 1) for i in range(frames - 1)]
    downward = [(i + 1, i) for i in range(frames - 1)]
    above = lax.ppermute(after, "frame", upward).astype(F32)
    below = lax.ppermute(before, "frame", downward).astype(F32)
    return base + above + below


def shards(kspace, sens, mask, image, w_first, b_first, w_mid, b_mid, w_last):
    frame, group = lax.axis_index("frame"), lax.axis_index("coil")
    frames, groups = lax.axis_size("frame"), lax.axis_size("coil")
    here = group.astype(jnp.int32)[None]
    x = data_step(image[0], kspace[0], sens, mask[0], here, groups)
    return denoise(x, w_first, b_first, w_mid, b_mid, w_last, frame, frames, group, groups)[None]


def solution(mesh):
    in_specs = (
        P("frame", "coil", None, None),
        P("coil", None, None),
        P("frame", "coil", None),
        P("frame", "coil", None),
        P(),
        P(),
        P(),
        P(),
        P(),
    )
    out_specs = P("frame", "coil", None)
    return jax.shard_map(shards, mesh=mesh, in_specs=in_specs, out_specs=out_specs, check_vma=False)
```

```python
import functools
import math

import jax
import jax.numpy as jnp
import numpy as np
from jax import lax
from jax.experimental import pallas as pl
from jax.experimental.pallas import tpu as pltpu
from jax.sharding import PartitionSpec as P

F32 = jnp.float32
BF16 = jnp.bfloat16

step_size = 1.0
RIM = 8
SLOT = 32


def dft_parts(order):
    indices = np.arange(order)
    angles = (indices[:, None] * indices[None, :] % order).astype(np.float32)
    angles = angles * np.float32(2.0 * math.pi / order)
    factor = np.float32(1.0 / math.sqrt(order))
    return np.stack([np.cos(angles) * factor, -np.sin(angles) * factor])


def put_table(ref, top_left, top_right, low_left, low_right):
    half = top_left.shape[0]
    ref[:half, :half] = top_left
    ref[:half, half:] = top_right
    ref[half:, :half] = low_left
    ref[half:, half:] = low_right


def halved(parts):
    short = parts.shape[1] // 2
    tables = []
    for real, imag in ((parts[0], parts[1]), (parts[0], -parts[1])):
        for odd in range(2):
            if len(tables) < 2:
                re, im = real[:short, odd::2], imag[:short, odd::2]
            else:
                re, im = real[odd::2, :short], imag[odd::2, :short]
            tables.append(
                np.concatenate([np.concatenate([re, -im], 1), np.concatenate([im, re], 1)], 0)
            )
    return np.stack(tables)


def data_kernel(
    coils_at_once,
    chunk,
    where_ref,
    image_ref,
    others_ref,
    kspace_ref,
    sens_ref,
    mask_ref,
    cols_ref,
    rows_ref,
    own_ref,
    send_ref,
    full_ref,
    acc_ref,
    natural_ref,
    smooth_ref,
    coil_ref,
    spec_ref,
    esti_ref,
    miss_ref,
    fold_ref,
    bimg_ref,
    col_ahead_ref,
    col_behind_ref,
):
    groups = others_ref.shape[0] + 1
    own_rows = image_ref.shape[0]
    n_rows, double = full_ref.shape
    half, short = double // 2, n_rows // 2
    lanes = double // 128
    me = where_ref[0]
    step = pl.program_id(0)

    @pl.when(step == 0)
    def _():
        real, imag = cols_ref[0], cols_ref[1]
        put_table(col_ahead_ref, real, imag, -imag, real)
        put_table(col_behind_ref, real, -imag, imag, real)
        acc_ref[...] = jnp.zeros_like(acc_ref)
        natural_ref[...] = jnp.zeros_like(natural_ref)
        for j in range(lanes):
            part = slice(j * 128, (j + 1) * 128)
            mine = pl.multiple_of(me * own_rows + RIM, RIM)
            natural_ref[j, pl.ds(mine, own_rows), :] = image_ref[:, part].astype(BF16).astype(F32)
            for hop in range(1, groups):
                theirs = lax.rem(me + groups - hop, groups) * own_rows + RIM
                natural_ref[j, pl.ds(pl.multiple_of(theirs, RIM), own_rows), :] = others_ref[
                    hop - 1, :, part
                ].astype(F32)
            for odd in range(2):
                full_ref[odd * short : (odd + 1) * short, part] = natural_ref[
                    j, pl.ds(RIM + odd, short, stride=2), :
                ]

    for coil in range(coils_at_once):
        for j in range(lanes):
            smooth_ref[coil, j] = sens_ref[coil, :, j * 128 : (j + 1) * 128].astype(F32)

    def maps(coil, odd, start):
        at = pl.ds(2 * start + odd, chunk, stride=2)
        pieces = [smooth_ref[coil, j, at, :] for j in range(lanes)]
        return (
            jnp.concatenate(pieces[: lanes // 2], 1),
            jnp.concatenate(pieces[lanes // 2 :], 1),
        )

    for odd in range(2):
        for start in range(0, short, chunk):
            place = odd * short + start
            rows = slice(place, place + chunk)
            x_re, x_im = full_ref[rows, :half], full_ref[rows, half:]
            for coil in range(coils_at_once):
                sens_re, sens_im = maps(coil, odd, start)
                out = slice(coil * n_rows + place, coil * n_rows + place + chunk)
                coil_ref[out, :half] = (sens_re * x_re - sens_im * x_im).astype(BF16)
                coil_ref[out, half:] = (sens_re * x_im + sens_im * x_re).astype(BF16)
    spec_ref[...] = jnp.dot(
        coil_ref[...], col_ahead_ref[...], preferred_element_type=F32
    ).astype(BF16)
    for coil in range(coils_at_once):
        for odd in range(2):
            at = coil * n_rows + odd * short
            stacked = jnp.concatenate(
                [spec_ref[at : at + short, :half], spec_ref[at : at + short, half:]], 0
            )
            esti_ref[coil, odd] = jnp.dot(rows_ref[odd], stacked, preferred_element_type=F32)
    for coil in range(coils_at_once):
        line = mask_ref[pl.ds(step * coils_at_once + coil, 1), :].astype(F32)
        sampled = jnp.broadcast_to(line, (128, n_rows)).T
        for start in range(0, short, chunk):
            for c in range(2):
                rows = slice(c * short + start, c * short + start + chunk)
                even, uneven = esti_ref[coil, 0, rows, :], esti_ref[coil, 1, rows, :]
                for upper, estimate in enumerate((even + uneven, even - uneven)):
                    at = slice(upper * short + start, upper * short + start + chunk)
                    taken = jnp.concatenate([sampled[at]] * (half // 128), 1)
                    part = slice(c * half, (c + 1) * half)
                    out = slice(
                        coil * n_rows + upper * short + start,
                        coil * n_rows + upper * short + start + chunk,
                    )
                    miss_ref[out, part] = (
                        taken * (estimate - kspace_ref[coil, at, part].astype(F32))
                    ).astype(BF16)
    for coil in range(coils_at_once):
        at = coil * n_rows
        lines = jnp.dot(
            miss_ref[at : at + n_rows, :], col_behind_ref[...], preferred_element_type=F32
        )
        for odd, folded in enumerate(
            (lines[:short] + lines[short:], lines[:short] - lines[short:])
        ):
            fold_ref[coil, odd, :short, :] = folded[:, :half].astype(BF16)
            fold_ref[coil, odd, short:, :] = folded[:, half:].astype(BF16)
    for coil in range(coils_at_once):
        for odd in range(2):
            bimg_ref[coil, odd] = jnp.dot(
                rows_ref[2 + odd], fold_ref[coil, odd], preferred_element_type=F32
            )
    for odd in range(2):
        for start in range(0, short, chunk):
            place = slice(odd * short + start, odd * short + start + chunk)
            rows, lower = slice(start, start + chunk), slice(short + start, short + start + chunk)
            total_re, total_im = acc_ref[place, :half], acc_ref[place, half:]
            for coil in range(coils_at_once):
                sens_re, sens_im = maps(coil, odd, start)
                back_re, back_im = bimg_ref[coil, odd, rows, :], bimg_ref[coil, odd, lower, :]
                total_re = total_re + (sens_re * back_re + sens_im * back_im)
                total_im = total_im + (sens_re * back_im - sens_im * back_re)
            acc_ref[place, :half] = total_re
            acc_ref[place, half:] = total_im

    @pl.when(step == pl.num_programs(0) - 1)
    def _():
        window = own_rows + 2 * RIM
        for j in range(lanes):
            part = slice(j * 128, (j + 1) * 128)
            for odd in range(2):
                natural_ref[j, pl.ds(RIM + odd, short, stride=2), :] = (
                    acc_ref[odd * short : (odd + 1) * short, part] * -step_size
                )
            mine = pl.ds(pl.multiple_of(me * own_rows + RIM, RIM), own_rows)
            natural_ref[j, mine, :] += image_ref[:, part]
            own_ref[:, part] = natural_ref[j, pl.ds(pl.multiple_of(me * own_rows, RIM), window), :]
            for hop in range(1, groups):
                theirs = pl.multiple_of(lax.rem(me + hop, groups) * own_rows, RIM)
                send_ref[hop - 1, :, part] = natural_ref[j, pl.ds(theirs, window), :].astype(BF16)


def data_step(image, kspace, sens, mask, here, groups):
    own_rows, double = image.shape
    coils, n_rows, _ = sens.shape
    half = double // 2
    coils_at_once = unrolled(coils, 4)
    shift = lambda hop: [(i, (i + hop) % groups) for i in range(groups)]
    low = image.astype(BF16)
    others = jnp.stack([lax.ppermute(low, "coil", shift(hop)) for hop in range(1, groups)])
    cols = jnp.asarray(dft_parts(half), BF16)
    lines = jnp.asarray(halved(dft_parts(n_rows)), BF16)
    window = own_rows + 2 * RIM
    vmem = pl.BlockSpec(memory_space=pltpu.VMEM)
    per_coil = lambda a: pl.BlockSpec(
        (coils_at_once,) + a.shape[1:], lambda i: (i,) + (0,) * (a.ndim - 1)
    )
    own, send = pl.pallas_call(
        functools.partial(data_kernel, coils_at_once, 32),
        grid=(coils // coils_at_once,),
        in_specs=[
            pl.BlockSpec(memory_space=pltpu.SMEM),
            vmem,
            vmem,
            per_coil(kspace),
            per_coil(sens),
            vmem,
            vmem,
            vmem,
        ],
        out_specs=[
            pl.BlockSpec((window, double), lambda i: (0, 0)),
            pl.BlockSpec((groups - 1, window, double), lambda i: (0, 0, 0)),
        ],
        out_shape=[
            jax.ShapeDtypeStruct((window, double), F32),
            jax.ShapeDtypeStruct((groups - 1, window, double), BF16),
        ],
        scratch_shapes=[
            pltpu.VMEM((n_rows, double), F32),
            pltpu.VMEM((n_rows, double), F32),
            pltpu.VMEM((double // 128, n_rows + 2 * RIM, 128), F32),
            pltpu.VMEM((coils_at_once, double // 128, n_rows, 128), F32),
            pltpu.VMEM((coils_at_once * n_rows, double), BF16),
            pltpu.VMEM((coils_at_once * n_rows, double), BF16),
            pltpu.VMEM((coils_at_once, 2, n_rows, half), F32),
            pltpu.VMEM((coils_at_once * n_rows, double), BF16),
            pltpu.VMEM((coils_at_once, 2, n_rows, half), BF16),
            pltpu.VMEM((coils_at_once, 2, n_rows, half), F32),
        ]
        + [pltpu.VMEM((double, double), BF16)] * 2,
        compiler_params=pltpu.CompilerParams(vmem_limit_bytes=57 << 20),
        cost_estimate=pl.CostEstimate(
            flops=32 * coils * n_rows * n_rows * half,
            bytes_accessed=4 * coils * n_rows * double,
            transcendentals=0,
        ),
        name="data_step",
    )(here, image, others, kspace, sens, mask, cols, lines)
    for hop in range(1, groups):
        own = own + lax.ppermute(send[hop - 1], "coil", shift(hop)).astype(F32)
    return own


def first_selector(channels_in):
    taps = 27 * channels_in
    select = np.zeros((4, 3, 64, 6 * SLOT), np.float32)
    for row in range(4):
        for frame in range(3):
            for a in range(3):
                for b in range(3):
                    for e in range(3):
                        for c in range(channels_in):
                            tap = ((a * 3 + b) * 3 + e) * channels_in + c
                            at = ((frame + a) * channels_in + c) * 3 + e
                            select[row, frame, tap, (row + b) * SLOT + at] = 1.0
            for part in range(3):
                at = (part // 2) * SLOT + SLOT - 2 + part % 2
                select[row, frame, taps + part, at] = 1.0
    return select.reshape(12, 64, 6 * SLOT)


def interleaver():
    order = np.zeros((8 * SLOT, 8 * SLOT), np.float32)
    for row in range(8):
        for plane in range(SLOT):
            order[row * SLOT + plane, plane * 8 + row] = 1.0
    return order


def last_selector():
    select = np.zeros((3, 3, 3, 2, 8, 54), np.float32)
    for b in range(3):
        for e in range(3):
            for a in range(3):
                for c in range(2):
                    select[b, e, a, c, :, ((a * 3 + b) * 3 + e) * 2 + c] = 1.0
    return select.reshape(432, 54)


def unrolled(count, at_most):
    return max(d for d in range(1, at_most + 1) if count % d == 0)


def shifted(values, amount):
    width = values.shape[-1]
    lane = lax.broadcasted_iota(jnp.int32, values.shape, 1)
    if amount > 0:
        return jnp.where(lane == 0, 0.0, pltpu.roll(values, 1, 1))
    return jnp.where(lane == width - 1, 0.0, pltpu.roll(values, width - 1, 1))


def denoise_kernel(
    groups,
    frames,
    group_ref,
    frame_ref,
    x_ref,
    hidden_ref,
    partner_ref,
    first_pair_ref,
    other_pair_ref,
    first_handed_ref,
    other_handed_ref,
    w1_ref,
    b1_ref,
    select_ref,
    order_ref,
    wmid_ref,
    bm_ref,
    wlast_ref,
    place_ref,
    inner_ref,
    base_ref,
    outer_ref,
    plane_ref,
    slab_ref,
    wide_ref,
    wm_ref,
    wl_ref,
    h1_ref,
    h2_ref,
):
    window, double = x_ref.shape
    half = double // 2
    rows = window - 2 * RIM
    out_chan = wmid_ref.shape[1]
    per_row = 3 * out_chan
    group, frame_now = group_ref[0], frame_ref[0]

    bias1 = b1_ref[...]
    high = bias1.astype(BF16).astype(F32)
    middle = (bias1 - high).astype(BF16).astype(F32)
    parts = [w1_ref[...].astype(F32), high, middle, bias1 - high - middle]
    spare = 64 - sum(part.shape[0] for part in parts)
    w1 = jnp.concatenate(parts + [jnp.zeros((spare, out_chan), F32)], 0).T.astype(BF16)
    inside = (frame_now > 0, None, frame_now < frames - 1)
    for row in range(4):
        for frame in range(3):
            band = jnp.dot(w1, select_ref[row * 3 + frame], preferred_element_type=F32)
            if inside[frame] is not None:
                band = band * jnp.where(inside[frame], 1.0, 0.0)
            at = (row * 3 + frame) * out_chan
            wide_ref[at : at + out_chan, :] = band.astype(BF16)
    nothing = jnp.zeros((out_chan, out_chan), BF16)
    for e in range(3):
        for row in range(2):
            blocks = [
                wmid_ref[(a * 3 + r - row) * 3 + e] if 0 <= r - row <= 2 else nothing
                for r in range(4)
                for a in range(3)
            ]
            at = (e * 2 + row) * out_chan
            wm_ref[at : at + out_chan, :] = jnp.concatenate(blocks, 1)
    picked = jnp.dot(place_ref[...], wlast_ref[...], preferred_element_type=F32)
    eight = lax.broadcasted_iota(jnp.int32, (144, out_chan), 0) & 7
    wl_ref[...] = jnp.concatenate(
        [
            sum(
                jnp.where(eight == r - b, picked[b * 144 : (b + 1) * 144], 0.0)
                for b in range(3)
            )
            for r in range(10)
        ],
        1,
    ).astype(BF16)
    odd_frame = frame_now & 1
    odd_pair = (frame_now >> 1) & 1
    handed_on = jnp.where(
        odd_frame == odd_pair,
        other_handed_ref[...].astype(F32),
        first_handed_ref[...].astype(F32),
    )
    for slot, frame_values in (
        (4 - 4 * odd_pair, first_pair_ref[...].astype(F32)),
        (3 - 2 * odd_frame, partner_ref[...].astype(F32)),
        (2, hidden_ref[...].astype(F32)),
        (1 + 2 * odd_frame, handed_on),
        (4 * odd_pair, other_pair_ref[...].astype(F32)),
    ):
        for c in range(2):
            plane = frame_values[:, c * half : (c + 1) * half]
            for e, moved in enumerate((shifted(plane, 1), plane, shifted(plane, -1))):
                plane_ref[(slot * 2 + c) * 3 + e] = moved
    ones = jnp.ones((16, half), F32)

    def interleave(block, carry):
        rows8 = pl.ds(pl.multiple_of(block * 8, 8), 8)
        planes = [plane_ref[k, rows8, :] for k in range(30)] + [ones]
        taps = jnp.concatenate(planes, 0).astype(BF16)
        made = jnp.dot(order_ref[...], taps, preferred_element_type=F32)
        slab_ref[pl.ds(pl.multiple_of(block * 8 * SLOT, 8 * SLOT), 8 * SLOT), :] = made.astype(BF16)
        return carry

    lax.fori_loop(0, window // 8, interleave, 0, unroll=unrolled(window // 8, 6))

    def first(q, carry):
        source = pl.multiple_of((4 * q + RIM - 3) * SLOT, SLOT)
        taps = slab_ref[pl.ds(source, 6 * SLOT), :]
        made = jnp.dot(wide_ref[...], taps, preferred_element_type=F32)
        target = pl.multiple_of(4 * q * per_row, per_row)
        h1_ref[pl.ds(target, 4 * per_row), :] = jnp.maximum(made, 0.0).astype(BF16)
        return carry

    lax.fori_loop(0, (rows + 4) // 4, first, 0, unroll=unrolled((rows + 4) // 4, 11))
    edge = jnp.zeros((2 * per_row, half), BF16)

    @pl.when(group == 0)
    def _():
        h1_ref[: 2 * per_row, :] = edge

    @pl.when(group == groups - 1)
    def _():
        h1_ref[(rows + 2) * per_row :, :] = edge

    both = 2 * out_chan
    bias = jnp.broadcast_to(bm_ref[...], (128, out_chan)).T
    bias = jnp.concatenate([bias] * 2, 0)
    bias = jnp.concatenate([bias] * (half // 128), 1)

    def mid(p, carry):
        source = pl.multiple_of(2 * p * per_row, 2 * per_row)
        taps = h1_ref[pl.ds(source, 4 * per_row), :]
        made = jnp.dot(wm_ref[...], taps, preferred_element_type=F32)
        total = (
            made[both : 2 * both]
            + shifted(made[:both], 1)
            + shifted(made[2 * both :], -1)
            + bias
        )
        target = pl.multiple_of(p * both, both)
        h2_ref[pl.ds(target, both), :] = jnp.maximum(total, 0.0).astype(BF16)
        return carry

    lax.fori_loop(0, (rows + 2) // 2, mid, 0, unroll=unrolled((rows + 2) // 2, 13))
    edge2 = jnp.zeros((out_chan, half), BF16)

    @pl.when(group == 0)
    def _():
        h2_ref[:out_chan, :] = edge2

    @pl.when(group == groups - 1)
    def _():
        h2_ref[(rows + 1) * out_chan :, :] = edge2

    def last(q, carry):
        source = pl.multiple_of(8 * q * out_chan, 8 * out_chan)
        taps = h2_ref[pl.ds(source, 10 * out_chan), :]
        made = jnp.dot(wl_ref[...], taps, preferred_element_type=F32)
        total = made[48:96] + shifted(made[:48], 1) + shifted(made[96:], -1)
        at = pl.ds(pl.multiple_of(8 * q, 8), 8)
        for c in range(2):
            lanes = slice(c * half, (c + 1) * half)
            piece = lambda a: total[(a * 2 + c) * 8 : (a * 2 + c) * 8 + 8]
            to_after, to_before = piece(0), piece(2)
            inner_ref[at, lanes] = jnp.where(odd_frame == 0, to_after, to_before).astype(BF16)
            outer_ref[at, lanes] = jnp.where(odd_frame == 0, to_before, to_after).astype(BF16)
            base_ref[at, lanes] = (
                x_ref[pl.ds(pl.multiple_of(8 * q + RIM, 8), 8), lanes] + piece(1)
            )
        return carry

    lax.fori_loop(0, rows // 8, last, 0, unroll=unrolled(rows // 8, 8))


def swaps(count, size, odd):
    ups = [(i, i + size) for i in range(count - size) if (i // size) % 2 == odd]
    return ups + [(j, i) for i, j in ups]


def denoise(x, w_first, b_first, w_mid, b_mid, w_last, frame, frames, group, groups):
    window, double = x.shape
    rows, half = window - 2 * RIM, double // 2
    out_chan = w_mid.shape[3]
    hidden = x.astype(BF16)
    within = swaps(frames, 1, 0)
    partner = lax.ppermute(hidden, "frame", within)
    first_pair = lax.ppermute(hidden, "frame", swaps(frames, 2, 0))
    other_pair = lax.ppermute(hidden, "frame", swaps(frames, 2, 1))
    first_handed = lax.ppermute(first_pair, "frame", within)
    other_handed = lax.ppermute(other_pair, "frame", within)
    near = (hidden, partner, first_pair, other_pair, first_handed, other_handed)
    weights = (
        jnp.transpose(w_first, (0, 1, 2, 4, 3)).reshape(-1, out_chan),
        b_first[None],
        jnp.asarray(first_selector(w_first.shape[4]), BF16),
        jnp.asarray(interleaver(), BF16),
        w_mid.reshape(-1, out_chan, out_chan),
        b_mid[None],
        w_last.reshape(-1, out_chan),
        jnp.asarray(last_selector(), BF16),
    )
    vmem = pl.BlockSpec(memory_space=pltpu.VMEM)
    smem = pl.BlockSpec(memory_space=pltpu.SMEM)
    out = lambda dtype: jax.ShapeDtypeStruct((rows, double), dtype)
    inner, base, outer = pl.pallas_call(
        functools.partial(denoise_kernel, groups, frames),
        in_specs=[smem] * 2 + [vmem] * 15,
        out_specs=[vmem] * 3,
        out_shape=[out(BF16), out(F32), out(BF16)],
        compiler_params=pltpu.CompilerParams(vmem_limit_bytes=44 << 20),
        scratch_shapes=[
            pltpu.VMEM((30, window, half), F32),
            pltpu.VMEM((window * SLOT, half), BF16),
            pltpu.VMEM((12 * out_chan, 6 * SLOT), BF16),
            pltpu.VMEM((6 * out_chan, 12 * out_chan), BF16),
            pltpu.VMEM((144, 10 * out_chan), BF16),
            pltpu.VMEM(((rows + 4) * 3 * out_chan, half), BF16),
            pltpu.VMEM(((rows + 2) * out_chan, half), BF16),
        ],
        cost_estimate=pl.CostEstimate(
            flops=2 * (rows + 2) * half * 192 * 1152,
            bytes_accessed=4 * window * double * 5,
            transcendentals=0,
        ),
        name="denoise",
    )(
        group.astype(jnp.int32)[None],
        frame.astype(jnp.int32)[None],
        x,
        *near,
        *weights,
    )
    across = swaps(frames, 1, 1)
    outer = lax.ppermute(outer, "frame", across).astype(F32)
    inner = lax.ppermute(inner, "frame", within).astype(F32)
    return base + inner + outer


def shards(kspace, sens, mask, image, w_first, b_first, w_mid, b_mid, w_last):
    frame, group = lax.axis_index("frame"), lax.axis_index("coil")
    frames, groups = lax.axis_size("frame"), lax.axis_size("coil")
    here = group.astype(jnp.int32)[None]
    x = data_step(image[0], kspace[0], sens, mask[0], here, groups)
    return denoise(x, w_first, b_first, w_mid, b_mid, w_last, frame, frames, group, groups)[None]


def solution(mesh):
    in_specs = (
        P("frame", "coil", None, None),
        P("coil", None, None),
        P("frame", "coil", None),
        P("frame", "coil", None),
        P(),
        P(),
        P(),
        P(),
        P(),
    )
    out_specs = P("frame", "coil", None)
    return jax.shard_map(shards, mesh=mesh, in_specs=in_specs, out_specs=out_specs, check_vma=False)
```

```python
import functools
import math

import jax
import jax.numpy as jnp
import numpy as np
from jax import lax
from jax.experimental import pallas as pl
from jax.experimental.pallas import tpu as pltpu
from jax.sharding import PartitionSpec as P

F32 = jnp.float32
BF16 = jnp.bfloat16

step_size = 1.0
RIM = 8
SLOT = 32


def dft_parts(order):
    indices = np.arange(order)
    angles = (indices[:, None] * indices[None, :] % order).astype(np.float32)
    angles = angles * np.float32(2.0 * math.pi / order)
    factor = np.float32(1.0 / math.sqrt(order))
    return np.stack([np.cos(angles) * factor, -np.sin(angles) * factor])


def put_table(ref, top_left, top_right, low_left, low_right):
    half = top_left.shape[0]
    ref[:half, :half] = top_left
    ref[:half, half:] = top_right
    ref[half:, :half] = low_left
    ref[half:, half:] = low_right


def halved(parts):
    short = parts.shape[1] // 2
    tables = []
    for real, imag in ((parts[0], parts[1]), (parts[0], -parts[1])):
        for odd in range(2):
            if len(tables) < 2:
                re, im = real[:short, odd::2], imag[:short, odd::2]
            else:
                re, im = real[odd::2, :short], imag[odd::2, :short]
            tables.append(
                np.concatenate([np.concatenate([re, -im], 1), np.concatenate([im, re], 1)], 0)
            )
    return np.stack(tables)


def data_kernel(
    coils_at_once,
    chunk,
    where_ref,
    image_ref,
    others_ref,
    kspace_ref,
    sens_ref,
    mask_ref,
    cols_ref,
    rows_ref,
    own_ref,
    send_ref,
    full_ref,
    acc_ref,
    natural_ref,
    smooth_ref,
    coil_ref,
    spec_ref,
    esti_ref,
    miss_ref,
    fold_ref,
    bimg_ref,
    col_ahead_ref,
    col_behind_ref,
):
    groups = others_ref.shape[0] + 1
    own_rows = image_ref.shape[0]
    n_rows, double = full_ref.shape
    half, short = double // 2, n_rows // 2
    lanes = double // 128
    me = where_ref[0]
    step = pl.program_id(0)

    @pl.when(step == 0)
    def _():
        real, imag = cols_ref[0], cols_ref[1]
        put_table(col_ahead_ref, real, imag, -imag, real)
        put_table(col_behind_ref, real, -imag, imag, real)
        acc_ref[...] = jnp.zeros_like(acc_ref)
        natural_ref[...] = jnp.zeros_like(natural_ref)
        for j in range(lanes):
            part = slice(j * 128, (j + 1) * 128)
            mine = pl.multiple_of(me * own_rows + RIM, RIM)
            natural_ref[j, pl.ds(mine, own_rows), :] = image_ref[:, part].astype(BF16).astype(F32)
            for hop in range(1, groups):
                theirs = lax.rem(me + groups - hop, groups) * own_rows + RIM
                natural_ref[j, pl.ds(pl.multiple_of(theirs, RIM), own_rows), :] = others_ref[
                    hop - 1, :, part
                ].astype(F32)
            for odd in range(2):
                full_ref[odd * short : (odd + 1) * short, part] = natural_ref[
                    j, pl.ds(RIM + odd, short, stride=2), :
                ]

    for coil in range(coils_at_once):
        for j in range(lanes):
            smooth_ref[coil, j] = sens_ref[coil, :, j * 128 : (j + 1) * 128].astype(F32)

    def maps(coil, odd, start):
        at = pl.ds(2 * start + odd, chunk, stride=2)
        pieces = [smooth_ref[coil, j, at, :] for j in range(lanes)]
        return (
            jnp.concatenate(pieces[: lanes // 2], 1),
            jnp.concatenate(pieces[lanes // 2 :], 1),
        )

    for odd in range(2):
        for start in range(0, short, chunk):
            place = odd * short + start
            rows = slice(place, place + chunk)
            x_re, x_im = full_ref[rows, :half], full_ref[rows, half:]
            for coil in range(coils_at_once):
                sens_re, sens_im = maps(coil, odd, start)
                out = slice(coil * n_rows + place, coil * n_rows + place + chunk)
                coil_ref[out, :half] = (sens_re * x_re - sens_im * x_im).astype(BF16)
                coil_ref[out, half:] = (sens_re * x_im + sens_im * x_re).astype(BF16)
    spec_ref[...] = jnp.dot(
        coil_ref[...], col_ahead_ref[...], preferred_element_type=F32
    ).astype(BF16)
    for coil in range(coils_at_once):
        for odd in range(2):
            at = coil * n_rows + odd * short
            stacked = jnp.concatenate(
                [spec_ref[at : at + short, :half], spec_ref[at : at + short, half:]], 0
            )
            esti_ref[coil, odd] = jnp.dot(rows_ref[odd], stacked, preferred_element_type=F32)
    for coil in range(coils_at_once):
        line = mask_ref[pl.ds(step * coils_at_once + coil, 1), :].astype(F32)
        sampled = jnp.broadcast_to(line, (128, n_rows)).T
        for start in range(0, short, chunk):
            for c in range(2):
                rows = slice(c * short + start, c * short + start + chunk)
                even, uneven = esti_ref[coil, 0, rows, :], esti_ref[coil, 1, rows, :]
                for upper, estimate in enumerate((even + uneven, even - uneven)):
                    at = slice(upper * short + start, upper * short + start + chunk)
                    taken = jnp.concatenate([sampled[at]] * (half // 128), 1)
                    part = slice(c * half, (c + 1) * half)
                    out = slice(
                        coil * n_rows + upper * short + start,
                        coil * n_rows + upper * short + start + chunk,
                    )
                    miss_ref[out, part] = (
                        taken * (estimate - kspace_ref[coil, at, part].astype(F32))
                    ).astype(BF16)
    for coil in range(coils_at_once):
        at = coil * n_rows
        lines = jnp.dot(
            miss_ref[at : at + n_rows, :], col_behind_ref[...], preferred_element_type=F32
        )
        for odd, folded in enumerate(
            (lines[:short] + lines[short:], lines[:short] - lines[short:])
        ):
            fold_ref[coil, odd, :short, :] = folded[:, :half].astype(BF16)
            fold_ref[coil, odd, short:, :] = folded[:, half:].astype(BF16)
    for coil in range(coils_at_once):
        for odd in range(2):
            bimg_ref[coil, odd] = jnp.dot(
                rows_ref[2 + odd], fold_ref[coil, odd], preferred_element_type=F32
            )
    for odd in range(2):
        for start in range(0, short, chunk):
            place = slice(odd * short + start, odd * short + start + chunk)
            rows, lower = slice(start, start + chunk), slice(short + start, short + start + chunk)
            total_re, total_im = acc_ref[place, :half], acc_ref[place, half:]
            for coil in range(coils_at_once):
                sens_re, sens_im = maps(coil, odd, start)
                back_re, back_im = bimg_ref[coil, odd, rows, :], bimg_ref[coil, odd, lower, :]
                total_re = total_re + (sens_re * back_re + sens_im * back_im)
                total_im = total_im + (sens_re * back_im - sens_im * back_re)
            acc_ref[place, :half] = total_re
            acc_ref[place, half:] = total_im

    @pl.when(step == pl.num_programs(0) - 1)
    def _():
        window = own_rows + 2 * RIM
        for j in range(lanes):
            part = slice(j * 128, (j + 1) * 128)
            for odd in range(2):
                natural_ref[j, pl.ds(RIM + odd, short, stride=2), :] = (
                    acc_ref[odd * short : (odd + 1) * short, part] * -step_size
                )
            mine = pl.ds(pl.multiple_of(me * own_rows + RIM, RIM), own_rows)
            natural_ref[j, mine, :] += image_ref[:, part]
            own_ref[:, part] = natural_ref[j, pl.ds(pl.multiple_of(me * own_rows, RIM), window), :]
            for hop in range(1, groups):
                theirs = pl.multiple_of(lax.rem(me + hop, groups) * own_rows, RIM)
                send_ref[hop - 1, :, part] = natural_ref[j, pl.ds(theirs, window), :].astype(BF16)


def data_step(image, kspace, sens, mask, here, groups):
    own_rows, double = image.shape
    coils, n_rows, _ = sens.shape
    half = double // 2
    coils_at_once = unrolled(coils, 4)
    shift = lambda hop: [(i, (i + hop) % groups) for i in range(groups)]
    low = image.astype(BF16)
    others = jnp.stack([lax.ppermute(low, "coil", shift(hop)) for hop in range(1, groups)])
    cols = jnp.asarray(dft_parts(half), BF16)
    lines = jnp.asarray(halved(dft_parts(n_rows)), BF16)
    window = own_rows + 2 * RIM
    vmem = pl.BlockSpec(memory_space=pltpu.VMEM)
    per_coil = lambda a: pl.BlockSpec(
        (coils_at_once,) + a.shape[1:], lambda i: (i,) + (0,) * (a.ndim - 1)
    )
    own, send = pl.pallas_call(
        functools.partial(data_kernel, coils_at_once, 32),
        grid=(coils // coils_at_once,),
        in_specs=[
            pl.BlockSpec(memory_space=pltpu.SMEM),
            vmem,
            vmem,
            per_coil(kspace),
            per_coil(sens),
            vmem,
            vmem,
            vmem,
        ],
        out_specs=[
            pl.BlockSpec((window, double), lambda i: (0, 0)),
            pl.BlockSpec((groups - 1, window, double), lambda i: (0, 0, 0)),
        ],
        out_shape=[
            jax.ShapeDtypeStruct((window, double), F32),
            jax.ShapeDtypeStruct((groups - 1, window, double), BF16),
        ],
        scratch_shapes=[
            pltpu.VMEM((n_rows, double), F32),
            pltpu.VMEM((n_rows, double), F32),
            pltpu.VMEM((double // 128, n_rows + 2 * RIM, 128), F32),
            pltpu.VMEM((coils_at_once, double // 128, n_rows, 128), F32),
            pltpu.VMEM((coils_at_once * n_rows, double), BF16),
            pltpu.VMEM((coils_at_once * n_rows, double), BF16),
            pltpu.VMEM((coils_at_once, 2, n_rows, half), F32),
            pltpu.VMEM((coils_at_once * n_rows, double), BF16),
            pltpu.VMEM((coils_at_once, 2, n_rows, half), BF16),
            pltpu.VMEM((coils_at_once, 2, n_rows, half), F32),
        ]
        + [pltpu.VMEM((double, double), BF16)] * 2,
        compiler_params=pltpu.CompilerParams(vmem_limit_bytes=57 << 20),
        cost_estimate=pl.CostEstimate(
            flops=32 * coils * n_rows * n_rows * half,
            bytes_accessed=4 * coils * n_rows * double,
            transcendentals=0,
        ),
        name="data_step",
    )(here, image, others, kspace, sens, mask, cols, lines)
    for hop in range(1, groups):
        own = own + lax.ppermute(send[hop - 1], "coil", shift(hop)).astype(F32)
    return own


def first_selector(channels_in):
    taps = 27 * channels_in
    select = np.zeros((4, 3, 64, 6 * SLOT), np.float32)
    for row in range(4):
        for frame in range(3):
            for a in range(3):
                for b in range(3):
                    for e in range(3):
                        for c in range(channels_in):
                            tap = ((a * 3 + b) * 3 + e) * channels_in + c
                            at = ((frame + a) * channels_in + c) * 3 + e
                            select[row, frame, tap, (row + b) * SLOT + at] = 1.0
            for part in range(3):
                at = (part // 2) * SLOT + SLOT - 2 + part % 2
                select[row, frame, taps + part, at] = 1.0
    return select.reshape(12, 64, 6 * SLOT)


def interleaver():
    order = np.zeros((8 * SLOT, 8 * SLOT), np.float32)
    for row in range(8):
        for plane in range(SLOT):
            order[row * SLOT + plane, plane * 8 + row] = 1.0
    return order


def last_selector():
    select = np.zeros((3, 3, 3, 2, 8, 54), np.float32)
    for b in range(3):
        for e in range(3):
            for a in range(3):
                for c in range(2):
                    select[b, e, a, c, :, ((a * 3 + b) * 3 + e) * 2 + c] = 1.0
    return select.reshape(432, 54)


def unrolled(count, at_most):
    return max(d for d in range(1, at_most + 1) if count % d == 0)


def shifted(values, amount):
    width = values.shape[-1]
    lane = lax.broadcasted_iota(jnp.int32, values.shape, 1)
    if amount > 0:
        return jnp.where(lane == 0, 0.0, pltpu.roll(values, 1, 1))
    return jnp.where(lane == width - 1, 0.0, pltpu.roll(values, width - 1, 1))


def denoise_kernel(
    groups,
    frames,
    group_ref,
    frame_ref,
    x_ref,
    hidden_ref,
    partner_ref,
    first_pair_ref,
    other_pair_ref,
    first_handed_ref,
    other_handed_ref,
    w1_ref,
    b1_ref,
    select_ref,
    order_ref,
    wmid_ref,
    bm_ref,
    wlast_ref,
    place_ref,
    inner_ref,
    base_ref,
    outer_ref,
    plane_ref,
    slab_ref,
    wide_ref,
    wm_ref,
    wl_ref,
    h1_ref,
    h2_ref,
):
    window, double = x_ref.shape
    half = double // 2
    rows = window - 2 * RIM
    out_chan = wmid_ref.shape[1]
    per_row = 3 * out_chan
    group, frame_now = group_ref[0], frame_ref[0]

    bias1 = b1_ref[...]
    high = bias1.astype(BF16).astype(F32)
    middle = (bias1 - high).astype(BF16).astype(F32)
    parts = [w1_ref[...].astype(F32), high, middle, bias1 - high - middle]
    spare = 64 - sum(part.shape[0] for part in parts)
    w1 = jnp.concatenate(parts + [jnp.zeros((spare, out_chan), F32)], 0).T.astype(BF16)
    inside = (frame_now > 0, None, frame_now < frames - 1)
    for row in range(4):
        for frame in range(3):
            band = jnp.dot(w1, select_ref[row * 3 + frame], preferred_element_type=F32)
            if inside[frame] is not None:
                band = band * jnp.where(inside[frame], 1.0, 0.0)
            at = (row * 3 + frame) * out_chan
            wide_ref[at : at + out_chan, :] = band.astype(BF16)
    nothing = jnp.zeros((out_chan, out_chan), BF16)
    for e in range(3):
        for row in range(2):
            blocks = [
                wmid_ref[(a * 3 + r - row) * 3 + e] if 0 <= r - row <= 2 else nothing
                for r in range(4)
                for a in range(3)
            ]
            at = (e * 2 + row) * out_chan
            wm_ref[at : at + out_chan, :] = jnp.concatenate(blocks, 1)
    picked = jnp.dot(place_ref[...], wlast_ref[...], preferred_element_type=F32)
    eight = lax.broadcasted_iota(jnp.int32, (144, out_chan), 0) & 7
    wl_ref[...] = jnp.concatenate(
        [
            sum(
                jnp.where(eight == r - b, picked[b * 144 : (b + 1) * 144], 0.0)
                for b in range(3)
            )
            for r in range(10)
        ],
        1,
    ).astype(BF16)
    odd_frame = frame_now & 1
    odd_pair = (frame_now >> 1) & 1
    handed_on = jnp.where(
        odd_frame == odd_pair,
        other_handed_ref[...].astype(F32),
        first_handed_ref[...].astype(F32),
    )
    for slot, frame_values in (
        (4 - 4 * odd_pair, first_pair_ref[...].astype(F32)),
        (3 - 2 * odd_frame, partner_ref[...].astype(F32)),
        (2, hidden_ref[...].astype(F32)),
        (1 + 2 * odd_frame, handed_on),
        (4 * odd_pair, other_pair_ref[...].astype(F32)),
    ):
        for c in range(2):
            plane = frame_values[:, c * half : (c + 1) * half]
            for e, moved in enumerate((shifted(plane, 1), plane, shifted(plane, -1))):
                plane_ref[(slot * 2 + c) * 3 + e] = moved
    ones = jnp.ones((16, half), F32)

    def interleave(block, carry):
        rows8 = pl.ds(pl.multiple_of(block * 8, 8), 8)
        planes = [plane_ref[k, rows8, :] for k in range(30)] + [ones]
        taps = jnp.concatenate(planes, 0).astype(BF16)
        made = jnp.dot(order_ref[...], taps, preferred_element_type=F32)
        slab_ref[pl.ds(pl.multiple_of(block * 8 * SLOT, 8 * SLOT), 8 * SLOT), :] = made.astype(BF16)
        return carry

    lax.fori_loop(0, window // 8, interleave, 0, unroll=unrolled(window // 8, 18))

    both = 2 * out_chan
    bias = jnp.broadcast_to(bm_ref[...], (128, out_chan)).T
    bias = jnp.concatenate([bias] * 2, 0)
    bias = jnp.concatenate([bias] * (half // 128), 1)

    def first(q):
        source = pl.multiple_of((4 * q + RIM - 3) * SLOT, SLOT)
        taps = slab_ref[pl.ds(source, 6 * SLOT), :]
        made = jnp.dot(wide_ref[...], taps, preferred_element_type=F32)
        target = pl.multiple_of((4 * q + 2) * per_row, 2 * per_row)
        h1_ref[pl.ds(target, 4 * per_row), :] = jnp.maximum(made, 0.0).astype(BF16)

    def mid(p):
        source = pl.multiple_of((2 * p + 2) * per_row, 2 * per_row)
        taps = h1_ref[pl.ds(source, 4 * per_row), :]
        made = jnp.dot(wm_ref[...], taps, preferred_element_type=F32)
        total = (
            made[both : 2 * both]
            + shifted(made[:both], 1)
            + shifted(made[2 * both :], -1)
            + bias
        )
        target = pl.multiple_of((p + 1) * both, both)
        h2_ref[pl.ds(target, both), :] = jnp.maximum(total, 0.0).astype(BF16)

    quads = (rows + 4) // 4
    some = unrolled(quads, 3)
    edge = jnp.zeros((2 * per_row, half), BF16)
    h1_ref[: 2 * per_row, :] = edge
    for q in range(some):
        first(q)

    @pl.when(group == 0)
    def _():
        h1_ref[2 * per_row : 4 * per_row, :] = edge

    def beside(g):
        for k in range(2 * some):
            mid(2 * some * (g - 1) - 1 + k)
        for k in range(some):
            first(some * g + k)

    for g in range(1, quads // some):
        beside(g)

    @pl.when(group == groups - 1)
    def _():
        h1_ref[(rows + 4) * per_row :, :] = edge

    for k in range(2 * some):
        mid(2 * (quads - some) - 1 + k)
    edge2 = jnp.zeros((out_chan, half), BF16)

    @pl.when(group == 0)
    def _():
        h2_ref[2 * out_chan : 3 * out_chan, :] = edge2

    @pl.when(group == groups - 1)
    def _():
        h2_ref[(rows + 3) * out_chan :, :] = edge2

    def last(q, carry):
        source = pl.multiple_of((8 * q + 2) * out_chan, 2 * out_chan)
        taps = h2_ref[pl.ds(source, 10 * out_chan), :]
        made = jnp.dot(wl_ref[...], taps, preferred_element_type=F32)
        total = made[48:96] + shifted(made[:48], 1) + shifted(made[96:], -1)
        at = pl.ds(pl.multiple_of(8 * q, 8), 8)
        for c in range(2):
            lanes = slice(c * half, (c + 1) * half)
            piece = lambda a: total[(a * 2 + c) * 8 : (a * 2 + c) * 8 + 8]
            to_after, to_before = piece(0), piece(2)
            inner_ref[at, lanes] = jnp.where(odd_frame == 0, to_after, to_before).astype(BF16)
            outer_ref[at, lanes] = jnp.where(odd_frame == 0, to_before, to_after).astype(BF16)
            base_ref[at, lanes] = (
                x_ref[pl.ds(pl.multiple_of(8 * q + RIM, 8), 8), lanes] + piece(1)
            )
        return carry

    lax.fori_loop(0, rows // 8, last, 0, unroll=unrolled(rows // 8, 16))


def swaps(count, size, odd):
    ups = [(i, i + size) for i in range(count - size) if (i // size) % 2 == odd]
    return ups + [(j, i) for i, j in ups]


def denoise(x, w_first, b_first, w_mid, b_mid, w_last, frame, frames, group, groups):
    window, double = x.shape
    rows, half = window - 2 * RIM, double // 2
    out_chan = w_mid.shape[3]
    hidden = x.astype(BF16)
    within = swaps(frames, 1, 0)
    partner = lax.ppermute(hidden, "frame", within)
    first_pair = lax.ppermute(hidden, "frame", swaps(frames, 2, 0))
    other_pair = lax.ppermute(hidden, "frame", swaps(frames, 2, 1))
    first_handed = lax.ppermute(first_pair, "frame", within)
    other_handed = lax.ppermute(other_pair, "frame", within)
    near = (hidden, partner, first_pair, other_pair, first_handed, other_handed)
    weights = (
        jnp.transpose(w_first, (0, 1, 2, 4, 3)).reshape(-1, out_chan),
        b_first[None],
        jnp.asarray(first_selector(w_first.shape[4]), BF16),
        jnp.asarray(interleaver(), BF16),
        w_mid.reshape(-1, out_chan, out_chan),
        b_mid[None],
        w_last.reshape(-1, out_chan),
        jnp.asarray(last_selector(), BF16),
    )
    vmem = pl.BlockSpec(memory_space=pltpu.VMEM)
    smem = pl.BlockSpec(memory_space=pltpu.SMEM)
    out = lambda dtype: jax.ShapeDtypeStruct((rows, double), dtype)
    inner, base, outer = pl.pallas_call(
        functools.partial(denoise_kernel, groups, frames),
        in_specs=[smem] * 2 + [vmem] * 15,
        out_specs=[vmem] * 3,
        out_shape=[out(BF16), out(F32), out(BF16)],
        compiler_params=pltpu.CompilerParams(vmem_limit_bytes=44 << 20),
        scratch_shapes=[
            pltpu.VMEM((30, window, half), F32),
            pltpu.VMEM((window * SLOT, half), BF16),
            pltpu.VMEM((12 * out_chan, 6 * SLOT), BF16),
            pltpu.VMEM((6 * out_chan, 12 * out_chan), BF16),
            pltpu.VMEM((144, 10 * out_chan), BF16),
            pltpu.VMEM(((rows + 6) * 3 * out_chan, half), BF16),
            pltpu.VMEM(((rows + 4) * out_chan, half), BF16),
        ],
        cost_estimate=pl.CostEstimate(
            flops=2 * (rows + 2) * half * 192 * 1152,
            bytes_accessed=4 * window * double * 5,
            transcendentals=0,
        ),
        name="denoise",
    )(
        group.astype(jnp.int32)[None],
        frame.astype(jnp.int32)[None],
        x,
        *near,
        *weights,
    )
    across = swaps(frames, 1, 1)
    outer = lax.ppermute(outer, "frame", across).astype(F32)
    inner = lax.ppermute(inner, "frame", within).astype(F32)
    return base + inner + outer


def shards(kspace, sens, mask, image, w_first, b_first, w_mid, b_mid, w_last):
    frame, group = lax.axis_index("frame"), lax.axis_index("coil")
    frames, groups = lax.axis_size("frame"), lax.axis_size("coil")
    here = group.astype(jnp.int32)[None]
    x = data_step(image[0], kspace[0], sens, mask[0], here, groups)
    return denoise(x, w_first, b_first, w_mid, b_mid, w_last, frame, frames, group, groups)[None]


def solution(mesh):
    in_specs = (
        P("frame", "coil", None, None),
        P("coil", None, None),
        P("frame", "coil", None),
        P("frame", "coil", None),
        P(),
        P(),
        P(),
        P(),
        P(),
    )
    out_specs = P("frame", "coil", None)
    return jax.shard_map(shards, mesh=mesh, in_specs=in_specs, out_specs=out_specs, check_vma=False)
```

```python
import functools
import math

import jax
import jax.numpy as jnp
import numpy as np
from jax import lax
from jax.experimental import pallas as pl
from jax.experimental.pallas import tpu as pltpu
from jax.sharding import PartitionSpec as P

F32 = jnp.float32
BF16 = jnp.bfloat16

step_size = 1.0
RIM = 8
SLOT = 32


def dft_parts(order):
    indices = np.arange(order)
    angles = (indices[:, None] * indices[None, :] % order).astype(np.float32)
    angles = angles * np.float32(2.0 * math.pi / order)
    factor = np.float32(1.0 / math.sqrt(order))
    return np.stack([np.cos(angles) * factor, -np.sin(angles) * factor])


def put_table(ref, top_left, top_right, low_left, low_right):
    half = top_left.shape[0]
    ref[:half, :half] = top_left
    ref[:half, half:] = top_right
    ref[half:, :half] = low_left
    ref[half:, half:] = low_right


def halved(parts):
    short = parts.shape[1] // 2
    tables = []
    for real, imag in ((parts[0], parts[1]), (parts[0], -parts[1])):
        for odd in range(2):
            if len(tables) < 2:
                re, im = real[:short, odd::2], imag[:short, odd::2]
            else:
                re, im = real[odd::2, :short], imag[odd::2, :short]
            tables.append(
                np.concatenate([np.concatenate([re, -im], 1), np.concatenate([im, re], 1)], 0)
            )
    return np.stack(tables)


def data_kernel(
    coils_at_once,
    chunk,
    where_ref,
    image_ref,
    others_ref,
    kspace_ref,
    sens_ref,
    mask_ref,
    col_ahead_ref,
    col_behind_ref,
    rows_ref,
    own_ref,
    send_ref,
    full_ref,
    acc_ref,
    natural_ref,
    smooth_ref,
    coil_ref,
    spec_ref,
    esti_ref,
    miss_ref,
    fold_ref,
    bimg_ref,
):
    groups = others_ref.shape[0] + 1
    own_rows = image_ref.shape[0]
    n_rows, double = full_ref.shape
    half, short = double // 2, n_rows // 2
    lanes = double // 128
    me = where_ref[0]
    step = pl.program_id(0)

    @pl.when(step == 0)
    def _():
        acc_ref[...] = jnp.zeros_like(acc_ref)
        natural_ref[...] = jnp.zeros_like(natural_ref)
        for j in range(lanes):
            part = slice(j * 128, (j + 1) * 128)
            mine = pl.multiple_of(me * own_rows + RIM, RIM)
            natural_ref[j, pl.ds(mine, own_rows), :] = image_ref[:, part].astype(BF16).astype(F32)
            for hop in range(1, groups):
                theirs = lax.rem(me + groups - hop, groups) * own_rows + RIM
                natural_ref[j, pl.ds(pl.multiple_of(theirs, RIM), own_rows), :] = others_ref[
                    hop - 1, :, part
                ].astype(F32)
            for odd in range(2):
                full_ref[odd * short : (odd + 1) * short, part] = natural_ref[
                    j, pl.ds(RIM + odd, short, stride=2), :
                ]

    for coil in range(coils_at_once):
        for j in range(lanes):
            smooth_ref[coil, j] = sens_ref[coil, :, j * 128 : (j + 1) * 128].astype(F32)

    def maps(coil, odd, start):
        at = pl.ds(2 * start + odd, chunk, stride=2)
        pieces = [smooth_ref[coil, j, at, :] for j in range(lanes)]
        return (
            jnp.concatenate(pieces[: lanes // 2], 1),
            jnp.concatenate(pieces[lanes // 2 :], 1),
        )

    for odd in range(2):
        for start in range(0, short, chunk):
            place = odd * short + start
            rows = slice(place, place + chunk)
            x_re, x_im = full_ref[rows, :half], full_ref[rows, half:]
            for coil in range(coils_at_once):
                sens_re, sens_im = maps(coil, odd, start)
                out = slice(coil * n_rows + place, coil * n_rows + place + chunk)
                coil_ref[out, :half] = (sens_re * x_re - sens_im * x_im).astype(BF16)
                coil_ref[out, half:] = (sens_re * x_im + sens_im * x_re).astype(BF16)
    spec_ref[...] = jnp.dot(
        coil_ref[...], col_ahead_ref[...], preferred_element_type=F32
    ).astype(BF16)
    for coil in range(coils_at_once):
        for odd in range(2):
            at = coil * n_rows + odd * short
            stacked = jnp.concatenate(
                [spec_ref[at : at + short, :half], spec_ref[at : at + short, half:]], 0
            )
            esti_ref[coil, odd] = jnp.dot(rows_ref[odd], stacked, preferred_element_type=F32)
    for coil in range(coils_at_once):
        line = mask_ref[pl.ds(step * coils_at_once + coil, 1), :].astype(F32)
        sampled = jnp.broadcast_to(line, (128, n_rows)).T
        for start in range(0, short, chunk):
            for c in range(2):
                rows = slice(c * short + start, c * short + start + chunk)
                even, uneven = esti_ref[coil, 0, rows, :], esti_ref[coil, 1, rows, :]
                for upper, estimate in enumerate((even + uneven, even - uneven)):
                    at = slice(upper * short + start, upper * short + start + chunk)
                    taken = jnp.concatenate([sampled[at]] * (half // 128), 1)
                    part = slice(c * half, (c + 1) * half)
                    out = slice(
                        coil * n_rows + upper * short + start,
                        coil * n_rows + upper * short + start + chunk,
                    )
                    miss_ref[out, part] = (
                        taken * (estimate - kspace_ref[coil, at, part].astype(F32))
                    ).astype(BF16)
    for coil in range(coils_at_once):
        at = coil * n_rows
        lines = jnp.dot(
            miss_ref[at : at + n_rows, :], col_behind_ref[...], preferred_element_type=F32
        )
        for odd, folded in enumerate(
            (lines[:short] + lines[short:], lines[:short] - lines[short:])
        ):
            fold_ref[coil, odd, :short, :] = folded[:, :half].astype(BF16)
            fold_ref[coil, odd, short:, :] = folded[:, half:].astype(BF16)
    for coil in range(coils_at_once):
        for odd in range(2):
            bimg_ref[coil, odd] = jnp.dot(
                rows_ref[2 + odd], fold_ref[coil, odd], preferred_element_type=F32
            )
    for odd in range(2):
        for start in range(0, short, chunk):
            place = slice(odd * short + start, odd * short + start + chunk)
            rows, lower = slice(start, start + chunk), slice(short + start, short + start + chunk)
            total_re, total_im = acc_ref[place, :half], acc_ref[place, half:]
            for coil in range(coils_at_once):
                sens_re, sens_im = maps(coil, odd, start)
                back_re, back_im = bimg_ref[coil, odd, rows, :], bimg_ref[coil, odd, lower, :]
                total_re = total_re + (sens_re * back_re + sens_im * back_im)
                total_im = total_im + (sens_re * back_im - sens_im * back_re)
            acc_ref[place, :half] = total_re
            acc_ref[place, half:] = total_im

    @pl.when(step == pl.num_programs(0) - 1)
    def _():
        window = own_rows + 2 * RIM
        for j in range(lanes):
            part = slice(j * 128, (j + 1) * 128)
            for odd in range(2):
                natural_ref[j, pl.ds(RIM + odd, short, stride=2), :] = (
                    acc_ref[odd * short : (odd + 1) * short, part] * -step_size
                )
            mine = pl.ds(pl.multiple_of(me * own_rows + RIM, RIM), own_rows)
            natural_ref[j, mine, :] += image_ref[:, part]
            own_ref[:, part] = natural_ref[j, pl.ds(pl.multiple_of(me * own_rows, RIM), window), :]
            for hop in range(1, groups):
                theirs = pl.multiple_of(lax.rem(me + hop, groups) * own_rows, RIM)
                send_ref[hop - 1, :, part] = natural_ref[j, pl.ds(theirs, window), :].astype(BF16)


def prepare_kernel(
    image_ref, mask_ref, cols_ref, image_out, mask_out, ahead_ref, behind_ref, parts_ref, sems
):
    copies = [
        pltpu.make_async_copy(source, target, sems.at[k])
        for k, (source, target) in enumerate(
            ((cols_ref, parts_ref), (image_ref, image_out), (mask_ref, mask_out))
        )
    ]
    for copy in copies:
        copy.start()
    copies[0].wait()
    real, imag = parts_ref[0], parts_ref[1]
    put_table(ahead_ref, real, imag, -imag, real)
    put_table(behind_ref, real, -imag, imag, real)
    copies[1].wait()
    copies[2].wait()


def data_step(image, kspace, sens, mask, here, groups):
    own_rows, double = image.shape
    coils, n_rows, _ = sens.shape
    half = double // 2
    coils_at_once = unrolled(coils, 4)
    shift = lambda hop: [(i, (i + hop) % groups) for i in range(groups)]
    low = image.astype(BF16)
    others = jnp.stack([lax.ppermute(low, "coil", shift(hop)) for hop in range(1, groups)])
    cols = jnp.asarray(dft_parts(half), BF16)
    lines = jnp.asarray(halved(dft_parts(n_rows)), BF16)
    table = jax.ShapeDtypeStruct((double, double), BF16)
    vmem = pl.BlockSpec(memory_space=pltpu.VMEM)
    image, mask, ahead, behind = pl.pallas_call(
        prepare_kernel,
        in_specs=[pl.BlockSpec(memory_space=pl.ANY)] * 3,
        out_specs=[vmem] * 4,
        out_shape=[jax.ShapeDtypeStruct(a.shape, a.dtype) for a in (image, mask)] + [table] * 2,
        scratch_shapes=[pltpu.VMEM(cols.shape, BF16), pltpu.SemaphoreType.DMA((3,))],
        compiler_params=pltpu.CompilerParams(vmem_limit_bytes=8 << 20),
        cost_estimate=pl.CostEstimate(flops=0, bytes_accessed=6 << 20, transcendentals=0),
        name="prepare",
    )(image, mask, cols)
    window = own_rows + 2 * RIM
    per_coil = lambda a: pl.BlockSpec(
        (coils_at_once,) + a.shape[1:], lambda i: (i,) + (0,) * (a.ndim - 1)
    )
    own, send = pl.pallas_call(
        functools.partial(data_kernel, coils_at_once, 32),
        grid=(coils // coils_at_once,),
        in_specs=[
            pl.BlockSpec(memory_space=pltpu.SMEM),
            vmem,
            vmem,
            per_coil(kspace),
            per_coil(sens),
            vmem,
            vmem,
            vmem,
            vmem,
        ],
        out_specs=[
            pl.BlockSpec((window, double), lambda i: (0, 0)),
            pl.BlockSpec((groups - 1, window, double), lambda i: (0, 0, 0)),
        ],
        out_shape=[
            jax.ShapeDtypeStruct((window, double), F32),
            jax.ShapeDtypeStruct((groups - 1, window, double), BF16),
        ],
        scratch_shapes=[
            pltpu.VMEM((n_rows, double), F32),
            pltpu.VMEM((n_rows, double), F32),
            pltpu.VMEM((double // 128, n_rows + 2 * RIM, 128), F32),
            pltpu.VMEM((coils_at_once, double // 128, n_rows, 128), F32),
            pltpu.VMEM((coils_at_once * n_rows, double), BF16),
            pltpu.VMEM((coils_at_once * n_rows, double), BF16),
            pltpu.VMEM((coils_at_once, 2, n_rows, half), F32),
            pltpu.VMEM((coils_at_once * n_rows, double), BF16),
            pltpu.VMEM((coils_at_once, 2, n_rows, half), BF16),
            pltpu.VMEM((coils_at_once, 2, n_rows, half), F32),
        ],
        compiler_params=pltpu.CompilerParams(vmem_limit_bytes=52 << 20),
        cost_estimate=pl.CostEstimate(
            flops=32 * coils * n_rows * n_rows * half,
            bytes_accessed=4 * coils * n_rows * double,
            transcendentals=0,
        ),
        name="data_step",
    )(here, image, others, kspace, sens, mask, ahead, behind, lines)
    for hop in range(1, groups):
        own = own + lax.ppermute(send[hop - 1], "coil", shift(hop)).astype(F32)
    return own


def first_selector(channels_in):
    taps = 27 * channels_in
    select = np.zeros((4, 3, 64, 6 * SLOT), np.float32)
    for row in range(4):
        for frame in range(3):
            for a in range(3):
                for b in range(3):
                    for e in range(3):
                        for c in range(channels_in):
                            tap = ((a * 3 + b) * 3 + e) * channels_in + c
                            at = ((frame + a) * channels_in + c) * 3 + e
                            select[row, frame, tap, (row + b) * SLOT + at] = 1.0
            for part in range(3):
                at = (part // 2) * SLOT + SLOT - 2 + part % 2
                select[row, frame, taps + part, at] = 1.0
    return select.reshape(12, 64, 6 * SLOT)


def interleaver():
    order = np.zeros((8 * SLOT, 8 * SLOT), np.float32)
    for row in range(8):
        for plane in range(SLOT):
            order[row * SLOT + plane, plane * 8 + row] = 1.0
    return order


def last_selector():
    select = np.zeros((3, 3, 3, 2, 8, 54), np.float32)
    for b in range(3):
        for e in range(3):
            for a in range(3):
                for c in range(2):
                    select[b, e, a, c, :, ((a * 3 + b) * 3 + e) * 2 + c] = 1.0
    return select.reshape(432, 54)


def unrolled(count, at_most):
    return max(d for d in range(1, at_most + 1) if count % d == 0)


def shifted(values, amount):
    width = values.shape[-1]
    lane = lax.broadcasted_iota(jnp.int32, values.shape, 1)
    if amount > 0:
        return jnp.where(lane == 0, 0.0, pltpu.roll(values, 1, 1))
    return jnp.where(lane == width - 1, 0.0, pltpu.roll(values, width - 1, 1))


def denoise_kernel(
    groups,
    frames,
    group_ref,
    frame_ref,
    x_ref,
    hidden_ref,
    partner_ref,
    first_pair_ref,
    other_pair_ref,
    first_handed_ref,
    other_handed_ref,
    w1_ref,
    b1_ref,
    select_ref,
    order_ref,
    wmid_ref,
    bm_ref,
    wlast_ref,
    place_ref,
    inner_ref,
    base_ref,
    outer_ref,
    plane_ref,
    slab_ref,
    wide_ref,
    wm_ref,
    wl_ref,
    h1_ref,
    h2_ref,
):
    window, double = x_ref.shape
    half = double // 2
    rows = window - 2 * RIM
    out_chan = wmid_ref.shape[1]
    per_row = 3 * out_chan
    group, frame_now = group_ref[0], frame_ref[0]

    bias1 = b1_ref[...]
    high = bias1.astype(BF16).astype(F32)
    middle = (bias1 - high).astype(BF16).astype(F32)
    parts = [w1_ref[...].astype(F32), high, middle, bias1 - high - middle]
    spare = 64 - sum(part.shape[0] for part in parts)
    w1 = jnp.concatenate(parts + [jnp.zeros((spare, out_chan), F32)], 0).T.astype(BF16)
    inside = (frame_now > 0, None, frame_now < frames - 1)
    for row in range(4):
        for frame in range(3):
            band = jnp.dot(w1, select_ref[row * 3 + frame], preferred_element_type=F32)
            if inside[frame] is not None:
                band = band * jnp.where(inside[frame], 1.0, 0.0)
            at = (row * 3 + frame) * out_chan
            wide_ref[at : at + out_chan, :] = band.astype(BF16)
    nothing = jnp.zeros((out_chan, out_chan), BF16)
    for e in range(3):
        for row in range(2):
            blocks = [
                wmid_ref[(a * 3 + r - row) * 3 + e] if 0 <= r - row <= 2 else nothing
                for r in range(4)
                for a in range(3)
            ]
            at = (e * 2 + row) * out_chan
            wm_ref[at : at + out_chan, :] = jnp.concatenate(blocks, 1)
    picked = jnp.dot(place_ref[...], wlast_ref[...], preferred_element_type=F32)
    eight = lax.broadcasted_iota(jnp.int32, (144, out_chan), 0) & 7
    wl_ref[...] = jnp.concatenate(
        [
            sum(
                jnp.where(eight == r - b, picked[b * 144 : (b + 1) * 144], 0.0)
                for b in range(3)
            )
            for r in range(10)
        ],
        1,
    ).astype(BF16)
    odd_frame = frame_now & 1
    odd_pair = (frame_now >> 1) & 1
    handed_on = jnp.where(
        odd_frame == odd_pair,
        other_handed_ref[...].astype(F32),
        first_handed_ref[...].astype(F32),
    )
    for slot, frame_values in (
        (4 - 4 * odd_pair, first_pair_ref[...].astype(F32)),
        (3 - 2 * odd_frame, partner_ref[...].astype(F32)),
        (2, hidden_ref[...].astype(F32)),
        (1 + 2 * odd_frame, handed_on),
        (4 * odd_pair, other_pair_ref[...].astype(F32)),
    ):
        for c in range(2):
            plane = frame_values[:, c * half : (c + 1) * half]
            for e, moved in enumerate((shifted(plane, 1), plane, shifted(plane, -1))):
                plane_ref[(slot * 2 + c) * 3 + e] = moved
    ones = jnp.ones((16, half), F32)

    def interleave(block, carry):
        rows8 = pl.ds(pl.multiple_of(block * 8, 8), 8)
        planes = [plane_ref[k, rows8, :] for k in range(30)] + [ones]
        taps = jnp.concatenate(planes, 0).astype(BF16)
        made = jnp.dot(order_ref[...], taps, preferred_element_type=F32)
        slab_ref[pl.ds(pl.multiple_of(block * 8 * SLOT, 8 * SLOT), 8 * SLOT), :] = made.astype(BF16)
        return carry

    lax.fori_loop(0, window // 8, interleave, 0, unroll=unrolled(window // 8, 18))

    both = 2 * out_chan
    bias = jnp.broadcast_to(bm_ref[...], (128, out_chan)).T
    bias = jnp.concatenate([bias] * 2, 0)
    bias = jnp.concatenate([bias] * (half // 128), 1)

    def first(q):
        source = pl.multiple_of((4 * q + RIM - 3) * SLOT, SLOT)
        taps = slab_ref[pl.ds(source, 6 * SLOT), :]
        made = jnp.dot(wide_ref[...], taps, preferred_element_type=F32)
        target = pl.multiple_of((4 * q + 2) * per_row, 2 * per_row)
        h1_ref[pl.ds(target, 4 * per_row), :] = jnp.maximum(made, 0.0).astype(BF16)

    def mid(p):
        source = pl.multiple_of((2 * p + 2) * per_row, 2 * per_row)
        taps = h1_ref[pl.ds(source, 4 * per_row), :]
        made = jnp.dot(wm_ref[...], taps, preferred_element_type=F32)
        total = (
            made[both : 2 * both]
            + shifted(made[:both], 1)
            + shifted(made[2 * both :], -1)
            + bias
        )
        target = pl.multiple_of((p + 1) * both, both)
        h2_ref[pl.ds(target, both), :] = jnp.maximum(total, 0.0).astype(BF16)

    quads = (rows + 4) // 4
    some = unrolled(quads, 3)
    edge = jnp.zeros((2 * per_row, half), BF16)
    h1_ref[: 2 * per_row, :] = edge
    for q in range(some):
        first(q)

    @pl.when(group == 0)
    def _():
        h1_ref[2 * per_row : 4 * per_row, :] = edge

    def beside(g):
        for k in range(2 * some):
            mid(2 * some * (g - 1) - 1 + k)
        for k in range(some):
            first(some * g + k)

    for g in range(1, quads // some):
        beside(g)

    @pl.when(group == groups - 1)
    def _():
        h1_ref[(rows + 4) * per_row :, :] = edge

    for k in range(2 * some):
        mid(2 * (quads - some) - 1 + k)
    edge2 = jnp.zeros((out_chan, half), BF16)

    @pl.when(group == 0)
    def _():
        h2_ref[2 * out_chan : 3 * out_chan, :] = edge2

    @pl.when(group == groups - 1)
    def _():
        h2_ref[(rows + 3) * out_chan :, :] = edge2

    def last(q, carry):
        source = pl.multiple_of((8 * q + 2) * out_chan, 2 * out_chan)
        taps = h2_ref[pl.ds(source, 10 * out_chan), :]
        made = jnp.dot(wl_ref[...], taps, preferred_element_type=F32)
        total = made[48:96] + shifted(made[:48], 1) + shifted(made[96:], -1)
        at = pl.ds(pl.multiple_of(8 * q, 8), 8)
        for c in range(2):
            lanes = slice(c * half, (c + 1) * half)
            piece = lambda a: total[(a * 2 + c) * 8 : (a * 2 + c) * 8 + 8]
            to_after, to_before = piece(0), piece(2)
            inner_ref[at, lanes] = jnp.where(odd_frame == 0, to_after, to_before).astype(BF16)
            outer_ref[at, lanes] = jnp.where(odd_frame == 0, to_before, to_after).astype(BF16)
            base_ref[at, lanes] = (
                x_ref[pl.ds(pl.multiple_of(8 * q + RIM, 8), 8), lanes] + piece(1)
            )
        return carry

    lax.fori_loop(0, rows // 8, last, 0, unroll=unrolled(rows // 8, 16))


def swaps(count, size, odd):
    ups = [(i, i + size) for i in range(count - size) if (i // size) % 2 == odd]
    return ups + [(j, i) for i, j in ups]


def denoise(x, w_first, b_first, w_mid, b_mid, w_last, frame, frames, group, groups):
    window, double = x.shape
    rows, half = window - 2 * RIM, double // 2
    out_chan = w_mid.shape[3]
    hidden = x.astype(BF16)
    within = swaps(frames, 1, 0)
    partner = lax.ppermute(hidden, "frame", within)
    first_pair = lax.ppermute(hidden, "frame", swaps(frames, 2, 0))
    other_pair = lax.ppermute(hidden, "frame", swaps(frames, 2, 1))
    first_handed = lax.ppermute(first_pair, "frame", within)
    other_handed = lax.ppermute(other_pair, "frame", within)
    near = (hidden, partner, first_pair, other_pair, first_handed, other_handed)
    weights = (
        jnp.transpose(w_first, (0, 1, 2, 4, 3)).reshape(-1, out_chan),
        b_first[None],
        jnp.asarray(first_selector(w_first.shape[4]), BF16),
        jnp.asarray(interleaver(), BF16),
        w_mid.reshape(-1, out_chan, out_chan),
        b_mid[None],
        w_last.reshape(-1, out_chan),
        jnp.asarray(last_selector(), BF16),
    )
    vmem = pl.BlockSpec(memory_space=pltpu.VMEM)
    smem = pl.BlockSpec(memory_space=pltpu.SMEM)
    out = lambda dtype: jax.ShapeDtypeStruct((rows, double), dtype)
    inner, base, outer = pl.pallas_call(
        functools.partial(denoise_kernel, groups, frames),
        in_specs=[smem] * 2 + [vmem] * 15,
        out_specs=[vmem] * 3,
        out_shape=[out(BF16), out(F32), out(BF16)],
        compiler_params=pltpu.CompilerParams(vmem_limit_bytes=44 << 20),
        scratch_shapes=[
            pltpu.VMEM((30, window, half), F32),
            pltpu.VMEM((window * SLOT, half), BF16),
            pltpu.VMEM((12 * out_chan, 6 * SLOT), BF16),
            pltpu.VMEM((6 * out_chan, 12 * out_chan), BF16),
            pltpu.VMEM((144, 10 * out_chan), BF16),
            pltpu.VMEM(((rows + 6) * 3 * out_chan, half), BF16),
            pltpu.VMEM(((rows + 4) * out_chan, half), BF16),
        ],
        cost_estimate=pl.CostEstimate(
            flops=2 * (rows + 2) * half * 192 * 1152,
            bytes_accessed=4 * window * double * 5,
            transcendentals=0,
        ),
        name="denoise",
    )(
        group.astype(jnp.int32)[None],
        frame.astype(jnp.int32)[None],
        x,
        *near,
        *weights,
    )
    across = swaps(frames, 1, 1)
    outer = lax.ppermute(outer, "frame", across).astype(F32)
    inner = lax.ppermute(inner, "frame", within).astype(F32)
    return base + inner + outer


def shards(kspace, sens, mask, image, w_first, b_first, w_mid, b_mid, w_last):
    frame, group = lax.axis_index("frame"), lax.axis_index("coil")
    frames, groups = lax.axis_size("frame"), lax.axis_size("coil")
    here = group.astype(jnp.int32)[None]
    x = data_step(image[0], kspace[0], sens, mask[0], here, groups)
    return denoise(x, w_first, b_first, w_mid, b_mid, w_last, frame, frames, group, groups)[None]


def solution(mesh):
    in_specs = (
        P("frame", "coil", None, None),
        P("coil", None, None),
        P("frame", "coil", None),
        P("frame", "coil", None),
        P(),
        P(),
        P(),
        P(),
        P(),
    )
    out_specs = P("frame", "coil", None)
    return jax.shard_map(shards, mesh=mesh, in_specs=in_specs, out_specs=out_specs, check_vma=False)
```

```python
import functools
import math

import jax
import jax.numpy as jnp
import numpy as np
from jax import lax
from jax.experimental import pallas as pl
from jax.experimental.pallas import tpu as pltpu
from jax.sharding import PartitionSpec as P

F32 = jnp.float32
BF16 = jnp.bfloat16

step_size = 1.0
RIM = 8
SLOT = 32


def dft_parts(order):
    indices = np.arange(order)
    angles = (indices[:, None] * indices[None, :] % order).astype(np.float32)
    angles = angles * np.float32(2.0 * math.pi / order)
    factor = np.float32(1.0 / math.sqrt(order))
    return np.stack([np.cos(angles) * factor, -np.sin(angles) * factor])


def put_table(ref, top_left, top_right, low_left, low_right):
    half = top_left.shape[0]
    ref[:half, :half] = top_left
    ref[:half, half:] = top_right
    ref[half:, :half] = low_left
    ref[half:, half:] = low_right


def halved(parts):
    short = parts.shape[1] // 2
    tables = []
    for real, imag in ((parts[0], parts[1]), (parts[0], -parts[1])):
        for odd in range(2):
            if len(tables) < 2:
                re, im = real[:short, odd::2], imag[:short, odd::2]
            else:
                re, im = real[odd::2, :short], imag[odd::2, :short]
            tables.append(
                np.concatenate([np.concatenate([re, -im], 1), np.concatenate([im, re], 1)], 0)
            )
    return np.stack(tables)


def data_kernel(
    coils_at_once,
    chunk,
    where_ref,
    image_ref,
    others_ref,
    kspace_ref,
    sens_ref,
    mask_ref,
    col_ahead_ref,
    col_behind_ref,
    rows_ref,
    own_ref,
    send_ref,
    full_ref,
    acc_ref,
    natural_ref,
    smooth_ref,
    coil_ref,
    spec_ref,
    esti_ref,
    miss_ref,
    fold_ref,
    bimg_ref,
):
    groups = others_ref.shape[0] + 1
    own_rows = image_ref.shape[0]
    n_rows, double = full_ref.shape
    half, short = double // 2, n_rows // 2
    lanes = double // 128
    me = where_ref[0]
    step = pl.program_id(0)

    @pl.when(step == 0)
    def _():
        acc_ref[...] = jnp.zeros_like(acc_ref)
        natural_ref[...] = jnp.zeros_like(natural_ref)
        for j in range(lanes):
            part = slice(j * 128, (j + 1) * 128)
            mine = pl.multiple_of(me * own_rows + RIM, RIM)
            natural_ref[j, pl.ds(mine, own_rows), :] = image_ref[:, part].astype(BF16).astype(F32)
            for hop in range(1, groups):
                theirs = lax.rem(me + groups - hop, groups) * own_rows + RIM
                natural_ref[j, pl.ds(pl.multiple_of(theirs, RIM), own_rows), :] = others_ref[
                    hop - 1, :, part
                ].astype(F32)
            for odd in range(2):
                full_ref[odd * short : (odd + 1) * short, part] = natural_ref[
                    j, pl.ds(RIM + odd, short, stride=2), :
                ]

    for coil in range(coils_at_once):
        for j in range(lanes):
            smooth_ref[coil, j] = sens_ref[coil, :, j * 128 : (j + 1) * 128].astype(F32)

    def maps(coil, odd, start):
        at = pl.ds(2 * start + odd, chunk, stride=2)
        pieces = [smooth_ref[coil, j, at, :] for j in range(lanes)]
        return (
            jnp.concatenate(pieces[: lanes // 2], 1),
            jnp.concatenate(pieces[lanes // 2 :], 1),
        )

    for odd in range(2):
        for start in range(0, short, chunk):
            place = odd * short + start
            rows = slice(place, place + chunk)
            x_re, x_im = full_ref[rows, :half], full_ref[rows, half:]
            for coil in range(coils_at_once):
                sens_re, sens_im = maps(coil, odd, start)
                out = slice(coil * n_rows + place, coil * n_rows + place + chunk)
                coil_ref[out, :half] = (sens_re * x_re - sens_im * x_im).astype(BF16)
                coil_ref[out, half:] = (sens_re * x_im + sens_im * x_re).astype(BF16)
    spec_ref[...] = jnp.dot(
        coil_ref[...], col_ahead_ref[...], preferred_element_type=F32
    ).astype(BF16)
    for coil in range(coils_at_once):
        for odd in range(2):
            at = coil * n_rows + odd * short
            stacked = jnp.concatenate(
                [spec_ref[at : at + short, :half], spec_ref[at : at + short, half:]], 0
            )
            esti_ref[coil, odd] = jnp.dot(rows_ref[odd], stacked, preferred_element_type=F32)
    for coil in range(coils_at_once):
        line = mask_ref[pl.ds(step * coils_at_once + coil, 1), :].astype(F32)
        sampled = jnp.broadcast_to(line, (128, n_rows)).T
        for start in range(0, short, chunk):
            for c in range(2):
                rows = slice(c * short + start, c * short + start + chunk)
                even, uneven = esti_ref[coil, 0, rows, :], esti_ref[coil, 1, rows, :]
                for upper, estimate in enumerate((even + uneven, even - uneven)):
                    at = slice(upper * short + start, upper * short + start + chunk)
                    taken = jnp.concatenate([sampled[at]] * (half // 128), 1)
                    part = slice(c * half, (c + 1) * half)
                    out = slice(
                        coil * n_rows + upper * short + start,
                        coil * n_rows + upper * short + start + chunk,
                    )
                    miss_ref[out, part] = (
                        taken * (estimate - kspace_ref[coil, at, part].astype(F32))
                    ).astype(BF16)
    for coil in range(coils_at_once):
        at = coil * n_rows
        lines = jnp.dot(
            miss_ref[at : at + n_rows, :], col_behind_ref[...], preferred_element_type=F32
        )
        for odd, folded in enumerate(
            (lines[:short] + lines[short:], lines[:short] - lines[short:])
        ):
            fold_ref[coil, odd, :short, :] = folded[:, :half].astype(BF16)
            fold_ref[coil, odd, short:, :] = folded[:, half:].astype(BF16)
    for coil in range(coils_at_once):
        for odd in range(2):
            bimg_ref[coil, odd] = jnp.dot(
                rows_ref[2 + odd], fold_ref[coil, odd], preferred_element_type=F32
            )
    for odd in range(2):
        for start in range(0, short, chunk):
            place = slice(odd * short + start, odd * short + start + chunk)
            rows, lower = slice(start, start + chunk), slice(short + start, short + start + chunk)
            total_re, total_im = acc_ref[place, :half], acc_ref[place, half:]
            for coil in range(coils_at_once):
                sens_re, sens_im = maps(coil, odd, start)
                back_re, back_im = bimg_ref[coil, odd, rows, :], bimg_ref[coil, odd, lower, :]
                total_re = total_re + (sens_re * back_re + sens_im * back_im)
                total_im = total_im + (sens_re * back_im - sens_im * back_re)
            acc_ref[place, :half] = total_re
            acc_ref[place, half:] = total_im

    @pl.when(step == pl.num_programs(0) - 1)
    def _():
        window = own_rows + 2 * RIM
        for j in range(lanes):
            part = slice(j * 128, (j + 1) * 128)
            for odd in range(2):
                natural_ref[j, pl.ds(RIM + odd, short, stride=2), :] = (
                    acc_ref[odd * short : (odd + 1) * short, part] * -step_size
                )
            mine = pl.ds(pl.multiple_of(me * own_rows + RIM, RIM), own_rows)
            natural_ref[j, mine, :] += image_ref[:, part]
            own_ref[:, part] = natural_ref[j, pl.ds(pl.multiple_of(me * own_rows, RIM), window), :]
            for hop in range(1, groups):
                theirs = pl.multiple_of(lax.rem(me + hop, groups) * own_rows, RIM)
                send_ref[hop - 1, :, part] = natural_ref[j, pl.ds(theirs, window), :].astype(BF16)


def prepare_kernel(
    image_ref, mask_ref, cols_ref, image_out, mask_out, ahead_ref, behind_ref, parts_ref, sems
):
    copies = [
        pltpu.make_async_copy(source, target, sems.at[k])
        for k, (source, target) in enumerate(
            ((cols_ref, parts_ref), (image_ref, image_out), (mask_ref, mask_out))
        )
    ]
    for copy in copies:
        copy.start()
    copies[0].wait()
    real, imag = parts_ref[0], parts_ref[1]
    put_table(ahead_ref, real, imag, -imag, real)
    put_table(behind_ref, real, -imag, imag, real)
    copies[1].wait()
    copies[2].wait()


def data_step(image, kspace, sens, mask, here, groups):
    own_rows, double = image.shape
    coils, n_rows, _ = sens.shape
    half = double // 2
    coils_at_once = unrolled(coils, 4)
    shift = lambda hop: [(i, (i + hop) % groups) for i in range(groups)]
    low = image.astype(BF16)
    others = jnp.stack([lax.ppermute(low, "coil", shift(hop)) for hop in range(1, groups)])
    cols = jnp.asarray(dft_parts(half), BF16)
    lines = jnp.asarray(halved(dft_parts(n_rows)), BF16)
    table = jax.ShapeDtypeStruct((double, double), BF16)
    vmem = pl.BlockSpec(memory_space=pltpu.VMEM)
    image, mask, ahead, behind = pl.pallas_call(
        prepare_kernel,
        in_specs=[pl.BlockSpec(memory_space=pl.ANY)] * 3,
        out_specs=[vmem] * 4,
        out_shape=[jax.ShapeDtypeStruct(a.shape, a.dtype) for a in (image, mask)] + [table] * 2,
        scratch_shapes=[pltpu.VMEM(cols.shape, BF16), pltpu.SemaphoreType.DMA((3,))],
        compiler_params=pltpu.CompilerParams(vmem_limit_bytes=8 << 20),
        cost_estimate=pl.CostEstimate(flops=0, bytes_accessed=6 << 20, transcendentals=0),
        name="prepare",
    )(image, mask, cols)
    window = own_rows + 2 * RIM
    per_coil = lambda a: pl.BlockSpec(
        (coils_at_once,) + a.shape[1:], lambda i: (i,) + (0,) * (a.ndim - 1)
    )
    own, send = pl.pallas_call(
        functools.partial(data_kernel, coils_at_once, 32),
        grid=(coils // coils_at_once,),
        in_specs=[
            pl.BlockSpec(memory_space=pltpu.SMEM),
            vmem,
            vmem,
            per_coil(kspace),
            per_coil(sens),
            vmem,
            vmem,
            vmem,
            vmem,
        ],
        out_specs=[
            pl.BlockSpec((window, double), lambda i: (0, 0)),
            pl.BlockSpec((groups - 1, window, double), lambda i: (0, 0, 0)),
        ],
        out_shape=[
            jax.ShapeDtypeStruct((window, double), F32),
            jax.ShapeDtypeStruct((groups - 1, window, double), BF16),
        ],
        scratch_shapes=[
            pltpu.VMEM((n_rows, double), F32),
            pltpu.VMEM((n_rows, double), F32),
            pltpu.VMEM((double // 128, n_rows + 2 * RIM, 128), F32),
            pltpu.VMEM((coils_at_once, double // 128, n_rows, 128), F32),
            pltpu.VMEM((coils_at_once * n_rows, double), BF16),
            pltpu.VMEM((coils_at_once * n_rows, double), BF16),
            pltpu.VMEM((coils_at_once, 2, n_rows, half), F32),
            pltpu.VMEM((coils_at_once * n_rows, double), BF16),
            pltpu.VMEM((coils_at_once, 2, n_rows, half), BF16),
            pltpu.VMEM((coils_at_once, 2, n_rows, half), F32),
        ],
        compiler_params=pltpu.CompilerParams(vmem_limit_bytes=52 << 20),
        cost_estimate=pl.CostEstimate(
            flops=32 * coils * n_rows * n_rows * half,
            bytes_accessed=4 * coils * n_rows * double,
            transcendentals=0,
        ),
        name="data_step",
    )(here, image, others, kspace, sens, mask, ahead, behind, lines)
    for hop in range(1, groups):
        own = own + lax.ppermute(send[hop - 1], "coil", shift(hop)).astype(F32)
    return own


def first_selector(channels_in):
    taps = 27 * channels_in
    select = np.zeros((4, 3, 64, 6 * SLOT), np.float32)
    for row in range(4):
        for frame in range(3):
            for a in range(3):
                for b in range(3):
                    for e in range(3):
                        for c in range(channels_in):
                            tap = ((a * 3 + b) * 3 + e) * channels_in + c
                            at = ((frame + a) * channels_in + c) * 3 + e
                            select[row, frame, tap, (row + b) * SLOT + at] = 1.0
            for part in range(3):
                at = (part // 2) * SLOT + SLOT - 2 + part % 2
                select[row, frame, taps + part, at] = 1.0
    return select.reshape(12, 64, 6 * SLOT)


def interleaver():
    order = np.zeros((8 * SLOT, 8 * SLOT), np.float32)
    for row in range(8):
        for plane in range(SLOT):
            order[row * SLOT + plane, plane * 8 + row] = 1.0
    return order


def last_selector():
    select = np.zeros((3, 3, 3, 2, 8, 54), np.float32)
    for b in range(3):
        for e in range(3):
            for a in range(3):
                for c in range(2):
                    select[b, e, a, c, :, ((a * 3 + b) * 3 + e) * 2 + c] = 1.0
    return select.reshape(432, 54)


def unrolled(count, at_most):
    return max(d for d in range(1, at_most + 1) if count % d == 0)


def shifted(values, amount):
    width = values.shape[-1]
    lane = lax.broadcasted_iota(jnp.int32, values.shape, 1)
    if amount > 0:
        return jnp.where(lane == 0, 0.0, pltpu.roll(values, 1, 1))
    return jnp.where(lane == width - 1, 0.0, pltpu.roll(values, width - 1, 1))


def denoise_kernel(
    groups,
    frames,
    group_ref,
    frame_ref,
    x_ref,
    hidden_ref,
    partner_ref,
    first_pair_ref,
    other_pair_ref,
    first_handed_ref,
    other_handed_ref,
    w1_ref,
    b1_ref,
    select_ref,
    order_ref,
    wmid_ref,
    bm_ref,
    wlast_ref,
    place_ref,
    outer_ref,
    base_ref,
    inner_ref,
    plane_ref,
    slab_ref,
    wide_ref,
    wm_ref,
    wl_ref,
    h1_ref,
    h2_ref,
):
    window, double = x_ref.shape
    half = double // 2
    rows = window - 2 * RIM
    out_chan = wmid_ref.shape[1]
    per_row = 3 * out_chan
    group, frame_now = group_ref[0], frame_ref[0]

    bias1 = b1_ref[...]
    high = bias1.astype(BF16).astype(F32)
    middle = (bias1 - high).astype(BF16).astype(F32)
    parts = [w1_ref[...].astype(F32), high, middle, bias1 - high - middle]
    spare = 64 - sum(part.shape[0] for part in parts)
    w1 = jnp.concatenate(parts + [jnp.zeros((spare, out_chan), F32)], 0).T.astype(BF16)
    inside = (frame_now > 0, None, frame_now < frames - 1)
    for row in range(4):
        for frame in range(3):
            band = jnp.dot(w1, select_ref[row * 3 + frame], preferred_element_type=F32)
            if inside[frame] is not None:
                band = band * jnp.where(inside[frame], 1.0, 0.0)
            at = (row * 3 + frame) * out_chan
            wide_ref[at : at + out_chan, :] = band.astype(BF16)
    nothing = jnp.zeros((out_chan, out_chan), BF16)
    for e in range(3):
        for row in range(2):
            blocks = [
                wmid_ref[(a * 3 + r - row) * 3 + e] if 0 <= r - row <= 2 else nothing
                for r in range(4)
                for a in range(3)
            ]
            at = (e * 2 + row) * out_chan
            wm_ref[at : at + out_chan, :] = jnp.concatenate(blocks, 1)
    picked = jnp.dot(place_ref[...], wlast_ref[...], preferred_element_type=F32)
    eight = lax.broadcasted_iota(jnp.int32, (144, out_chan), 0) & 7
    wl_ref[...] = jnp.concatenate(
        [
            sum(
                jnp.where(eight == r - b, picked[b * 144 : (b + 1) * 144], 0.0)
                for b in range(3)
            )
            for r in range(10)
        ],
        1,
    ).astype(BF16)
    odd_frame = frame_now & 1
    odd_pair = (frame_now >> 1) & 1
    handed_on = jnp.where(
        odd_frame == odd_pair,
        other_handed_ref[...].astype(F32),
        first_handed_ref[...].astype(F32),
    )
    for slot, frame_values in (
        (4 - 4 * odd_pair, first_pair_ref[...].astype(F32)),
        (3 - 2 * odd_frame, partner_ref[...].astype(F32)),
        (2, hidden_ref[...].astype(F32)),
        (1 + 2 * odd_frame, handed_on),
        (4 * odd_pair, other_pair_ref[...].astype(F32)),
    ):
        for c in range(2):
            plane = frame_values[:, c * half : (c + 1) * half]
            for e, moved in enumerate((shifted(plane, 1), plane, shifted(plane, -1))):
                plane_ref[(slot * 2 + c) * 3 + e] = moved
    ones = jnp.ones((16, half), F32)

    def interleave(block, carry):
        rows8 = pl.ds(pl.multiple_of(block * 8, 8), 8)
        planes = [plane_ref[k, rows8, :] for k in range(30)] + [ones]
        taps = jnp.concatenate(planes, 0).astype(BF16)
        made = jnp.dot(order_ref[...], taps, preferred_element_type=F32)
        slab_ref[pl.ds(pl.multiple_of(block * 8 * SLOT, 8 * SLOT), 8 * SLOT), :] = made.astype(BF16)
        return carry

    lax.fori_loop(0, window // 8, interleave, 0, unroll=unrolled(window // 8, 18))

    both = 2 * out_chan
    bias = jnp.broadcast_to(bm_ref[...], (128, out_chan)).T
    bias = jnp.concatenate([bias] * 2, 0)
    bias = jnp.concatenate([bias] * (half // 128), 1)

    def first(q):
        source = pl.multiple_of((4 * q + RIM - 3) * SLOT, SLOT)
        taps = slab_ref[pl.ds(source, 6 * SLOT), :]
        made = jnp.dot(wide_ref[...], taps, preferred_element_type=F32)
        target = pl.multiple_of((4 * q + 2) * per_row, 2 * per_row)
        h1_ref[pl.ds(target, 4 * per_row), :] = jnp.maximum(made, 0.0).astype(BF16)

    def mid(p):
        source = pl.multiple_of((2 * p + 2) * per_row, 2 * per_row)
        taps = h1_ref[pl.ds(source, 4 * per_row), :]
        made = jnp.dot(wm_ref[...], taps, preferred_element_type=F32)
        total = (
            made[both : 2 * both]
            + shifted(made[:both], 1)
            + shifted(made[2 * both :], -1)
            + bias
        )
        target = pl.multiple_of((p + 1) * both, both)
        h2_ref[pl.ds(target, both), :] = jnp.maximum(total, 0.0).astype(BF16)

    quads = (rows + 4) // 4
    some = unrolled(quads, 3)
    edge = jnp.zeros((2 * per_row, half), BF16)
    h1_ref[: 2 * per_row, :] = edge
    for q in range(some):
        first(q)

    @pl.when(group == 0)
    def _():
        h1_ref[2 * per_row : 4 * per_row, :] = edge

    def beside(g):
        for k in range(2 * some):
            mid(2 * some * (g - 1) - 1 + k)
        for k in range(some):
            first(some * g + k)

    for g in range(1, quads // some):
        beside(g)

    @pl.when(group == groups - 1)
    def _():
        h1_ref[(rows + 4) * per_row :, :] = edge

    for k in range(2 * some):
        mid(2 * (quads - some) - 1 + k)
    edge2 = jnp.zeros((out_chan, half), BF16)

    @pl.when(group == 0)
    def _():
        h2_ref[2 * out_chan : 3 * out_chan, :] = edge2

    @pl.when(group == groups - 1)
    def _():
        h2_ref[(rows + 3) * out_chan :, :] = edge2

    def last(q, carry):
        source = pl.multiple_of((8 * q + 2) * out_chan, 2 * out_chan)
        taps = h2_ref[pl.ds(source, 10 * out_chan), :]
        made = jnp.dot(wl_ref[...], taps, preferred_element_type=F32)
        total = made[48:96] + shifted(made[:48], 1) + shifted(made[96:], -1)
        at = pl.ds(pl.multiple_of(8 * q, 8), 8)
        for c in range(2):
            lanes = slice(c * half, (c + 1) * half)
            piece = lambda a: total[(a * 2 + c) * 8 : (a * 2 + c) * 8 + 8]
            to_after, to_before = piece(0), piece(2)
            inner_ref[at, lanes] = jnp.where(odd_frame == 0, to_after, to_before).astype(BF16)
            outer_ref[at, lanes] = jnp.where(odd_frame == 0, to_before, to_after).astype(BF16)
            base_ref[at, lanes] = (
                x_ref[pl.ds(pl.multiple_of(8 * q + RIM, 8), 8), lanes] + piece(1)
            )
        return carry

    lax.fori_loop(0, rows // 8, last, 0, unroll=unrolled(rows // 8, 16))


def swaps(count, size, odd):
    ups = [(i, i + size) for i in range(count - size) if (i // size) % 2 == odd]
    return ups + [(j, i) for i, j in ups]


def denoise(x, w_first, b_first, w_mid, b_mid, w_last, frame, frames, group, groups):
    window, double = x.shape
    rows, half = window - 2 * RIM, double // 2
    out_chan = w_mid.shape[3]
    hidden = x.astype(BF16)
    within = swaps(frames, 1, 0)
    partner = lax.ppermute(hidden, "frame", within)
    first_pair = lax.ppermute(hidden, "frame", swaps(frames, 2, 0))
    other_pair = lax.ppermute(hidden, "frame", swaps(frames, 2, 1))
    first_handed = lax.ppermute(first_pair, "frame", within)
    other_handed = lax.ppermute(other_pair, "frame", within)
    near = (hidden, partner, first_pair, other_pair, first_handed, other_handed)
    weights = (
        jnp.transpose(w_first, (0, 1, 2, 4, 3)).reshape(-1, out_chan),
        b_first[None],
        jnp.asarray(first_selector(w_first.shape[4]), BF16),
        jnp.asarray(interleaver(), BF16),
        w_mid.reshape(-1, out_chan, out_chan),
        b_mid[None],
        w_last.reshape(-1, out_chan),
        jnp.asarray(last_selector(), BF16),
    )
    vmem = pl.BlockSpec(memory_space=pltpu.VMEM)
    smem = pl.BlockSpec(memory_space=pltpu.SMEM)
    out = lambda dtype: jax.ShapeDtypeStruct((rows, double), dtype)
    outer, base, inner = pl.pallas_call(
        functools.partial(denoise_kernel, groups, frames),
        in_specs=[smem] * 2 + [vmem] * 15,
        out_specs=[vmem] * 3,
        out_shape=[out(BF16), out(F32), out(BF16)],
        compiler_params=pltpu.CompilerParams(vmem_limit_bytes=44 << 20),
        scratch_shapes=[
            pltpu.VMEM((30, window, half), F32),
            pltpu.VMEM((window * SLOT, half), BF16),
            pltpu.VMEM((12 * out_chan, 6 * SLOT), BF16),
            pltpu.VMEM((6 * out_chan, 12 * out_chan), BF16),
            pltpu.VMEM((144, 10 * out_chan), BF16),
            pltpu.VMEM(((rows + 6) * 3 * out_chan, half), BF16),
            pltpu.VMEM(((rows + 4) * out_chan, half), BF16),
        ],
        cost_estimate=pl.CostEstimate(
            flops=2 * (rows + 2) * half * 192 * 1152,
            bytes_accessed=4 * window * double * 5,
            transcendentals=0,
        ),
        name="denoise",
    )(
        group.astype(jnp.int32)[None],
        frame.astype(jnp.int32)[None],
        x,
        *near,
        *weights,
    )
    across = swaps(frames, 1, 1)
    outer = lax.ppermute(outer, "frame", across)
    inner = lax.ppermute(inner, "frame", within).astype(F32)
    outer = outer.astype(F32)
    return base + outer + inner


def shards(kspace, sens, mask, image, w_first, b_first, w_mid, b_mid, w_last):
    frame, group = lax.axis_index("frame"), lax.axis_index("coil")
    frames, groups = lax.axis_size("frame"), lax.axis_size("coil")
    here = group.astype(jnp.int32)[None]
    x = data_step(image[0], kspace[0], sens, mask[0], here, groups)
    return denoise(x, w_first, b_first, w_mid, b_mid, w_last, frame, frames, group, groups)[None]


def solution(mesh):
    in_specs = (
        P("frame", "coil", None, None),
        P("coil", None, None),
        P("frame", "coil", None),
        P("frame", "coil", None),
        P(),
        P(),
        P(),
        P(),
        P(),
    )
    out_specs = P("frame", "coil", None)
    return jax.shard_map(shards, mesh=mesh, in_specs=in_specs, out_specs=out_specs, check_vma=False)
```
